256 devices in a mesh: boson: 64 (over z, x, core), block: 4 (over y).
Axes of the slice: x: 4, y: 4, z: 8, core: 2. Of those that a mesh axis runs over, the one named last changes fastest.
Arguments:
- gamma_ph: bfloat16 [256, 1024, 1024], P('boson', 'block'), may hold values from -6 to 6
- full_ph: bfloat16 [256, 1024, 1024], P('boson', 'block'), may hold values from -0.1875 to 0.1875
- chi_ph: float32 [256, 1024], P('boson'), may hold values from 0.3 to 3
- pp_vertex: bfloat16 [256, 1024, 1024], P('boson', 'block'), may hold values from -0.1875 to 0.1875
- chi_pp: float32 [256, 1024], P('boson'), may hold values from 0.3 to 3
- relabel: int32 [256, 16, 8], replicated, may hold values from 0 to 255, as said below
Outputs:
- vertex_new: bfloat16 [256, 1024, 1024], P('boson', 'block')
The draws below stay inside these ranges and needn't reach their ends.
Inputs may be any that keep to these rules, and one draw needn't show every extreme that they name: `relabel`: for each row tile and column block the table is a permutation of the 256 points. The owner of the target point (target // 4) is the source's owner (q // 4) plus a shift modulo 64, and both this shift and the target's position among its owner's points (target % 4) depend only on the row tile, the column block and q % 4. Row tiles b * 4 to (b + 1) * 4 - 1 form row block b; within one row block, at most 3 of the 128 triples of position, row tile and column block share a shift, and some shift is shared by exactly 3; in every row block the shifts 1, 32 and 63 each occur.
All inputs are finite; a program needn't handle non-finite values.
Results may differ from the reference program's by a relative error of at most 0.0063.
Values may be sent and summed in bfloat16 or wider, within the bound.
No kernel may reach another device: no remote copies, remote signals or barrier semaphores. Data moves between devices by JAX's collectives and lax.ppermute only.
A program may use at most 128 MiB of HBM per device.

```python
import math
import jax
import jax.numpy as jnp
from jax import lax

M = 1024
CB = 8
RS = 4
RB = 16
QD = 4
QB = 256
CAP = 3
N_BOSON = 64
N_BLOCK = 4


def draw_relabel(key, part):
    item_total = QD * RS * CB
    blocks = []
    values = jnp.arange(N_BOSON, dtype=jnp.int32)
    for row_block in range(N_BLOCK):
        block_key = jax.random.fold_in(key, 101 + row_block)
        key_offset, key_mix, key_slot = jax.random.split(block_key, 3)
        ranks = jax.random.permutation(key_offset, N_BOSON).astype(jnp.int32) + 3
        ranks = jnp.where(values == 1, 0, ranks)
        ranks = jnp.where(values == N_BOSON // 2, 1, ranks)
        ranks = jnp.where(values == N_BOSON - 1, 2, ranks)
        shuffled = jnp.argsort(ranks, stable=True).astype(jnp.int32)
        spread = shuffled[jnp.arange(item_total) // CAP]
        spread = spread[jax.random.permutation(key_mix, item_total)].reshape(QD, RS * CB)
        position = jax.vmap(lambda subkey: jax.random.permutation(subkey, QD))(jax.random.split(key_slot, RS * CB)).T
        source = jnp.arange(N_BOSON, dtype=jnp.int32)[:, None, None]
        target_point = (source + spread[None]) % N_BOSON * QD + position[None]
        blocks.append(target_point.reshape(N_BOSON * QD, RS, CB).astype(jnp.int32))
    return jnp.stack(blocks, axis=1).reshape(N_BOSON * QD, RS * N_BLOCK, CB)


def steps_of(key, shape, cuts, smallest, top_value):
    factor_of = 1.0
    for dim, parts in cuts:
        heights = jax.random.uniform(jax.random.fold_in(jax.random.fold_in(key, 6), dim), (parts,), jnp.float32, smallest / len(cuts), top_value / len(cuts))
        factor_of = factor_of * jnp.repeat(jnp.exp(heights), shape[dim] // parts).reshape((-1,) + (1,) * (len(shape) - 1 - dim))
    return factor_of


def scatter_about(key, extent, deviation, reach, cuts=(), kind=jnp.bfloat16):
    array = jax.random.normal(key, extent, jnp.float32) * deviation
    if len(cuts) > 0:
        array = steps_of(key, extent, cuts, -0.22, 0.18) * array
    return jnp.clip(array, min=-reach, max=reach).astype(kind)


def setup_inputs(seed: int = 0) -> dict:
    arg_keys = jax.random.split(jax.random.key(seed), 7)
    gamma_ph = scatter_about(arg_keys[0], (QB, M, M), 1.0, 6.0, ((0, 64), (1, 4)))
    full_ph = scatter_about(arg_keys[1], (QB, M, M), M ** -0.5, 0.1875, ((0, 64), (1, 4)))
    chi_ph = jnp.clip(jnp.exp(math.log(3.0) - 2.3025851 * jax.random.uniform(arg_keys[2], (QB, M), jnp.float32) ** steps_of(arg_keys[2], (QB, M), ((0, 64),), -0.2, 0.2)), 0.3, 3.0)
    pp_vertex = scatter_about(arg_keys[3], (QB, M, M), M ** -0.5, 0.1875, ((0, 64), (1, 4)))
    chi_pp = jnp.clip(jnp.exp(math.log(3.0) - 2.3025851 * jax.random.uniform(arg_keys[4], (QB, M), jnp.float32) ** steps_of(arg_keys[4], (QB, M), ((0, 64),), -0.2, 0.2)), 0.3, 3.0)
    relabel = draw_relabel(jax.random.fold_in(arg_keys[6], 71), 0)
    return {"gamma_ph": gamma_ph, "full_ph": full_ph, "chi_ph": chi_ph, "pp_vertex": pp_vertex, "chi_pp": chi_pp, "relabel": relabel}


def to_tiles(matrix):
    return matrix.reshape(QB, RB, M // RB, CB, M // CB).transpose(0, 1, 3, 2, 4)


def from_tiles(tile_stack):
    return tile_stack.transpose(0, 1, 3, 2, 4).reshape(QB, M, M)


def bubble_product(left_side, column_scale, right_side):
    def single(inputs):
        left_one, scale_one, right_one = inputs
        scaled = (left_one.astype(jnp.float32) * scale_one[None, :]).astype(jnp.bfloat16)
        return jnp.dot(scaled, right_one, preferred_element_type=jnp.float32)
    return lax.map(single, (left_side, column_scale, right_side))


def reference(gamma_ph, full_ph, chi_ph, pp_vertex, chi_pp, relabel):
    phi_ph = bubble_product(gamma_ph, chi_ph, full_ph)
    ph_tiles = to_tiles(phi_ph.astype(jnp.bfloat16))
    row_index = jnp.broadcast_to(jnp.arange(RB, dtype=jnp.int32)[None, :, None], relabel.shape)
    col_index = jnp.broadcast_to(jnp.arange(CB, dtype=jnp.int32)[None, None, :], relabel.shape)
    pp_tiles = jnp.zeros_like(ph_tiles).at[relabel, row_index, col_index].set(ph_tiles)
    relabelled = from_tiles(pp_tiles)
    phi_pp = bubble_product(relabelled, chi_pp, pp_vertex).astype(jnp.bfloat16)
    returned = to_tiles(phi_pp)[relabel, row_index, col_index]
    vertex_new = gamma_ph.astype(jnp.float32) + phi_ph + from_tiles(returned).astype(jnp.float32)
    return vertex_new.astype(jnp.bfloat16)
```

```python
import jax
import jax.numpy as jnp
from jax import lax
from jax.experimental import pallas as pl
from jax.experimental.pallas import tpu as pltpu
from jax.sharding import PartitionSpec as P

CB = 8
RS = 4
CAP = 3
MIB = 1 << 20


def block_rows(shard, after=None):
    n = lax.axis_size("block")
    up = [(i, (i + 1) % n) for i in range(n)]
    down = [(i, (i - 1) % n) for i in range(n)]
    half = shard.shape[1] // 2
    from_below = lax.ppermute(shard, "block", up)
    from_above = lax.ppermute(shard, "block", down)
    far_low = lax.ppermute(from_below[:, :half], "block", up)
    far_high = lax.ppermute(from_above[:, half:], "block", down)
    return shard, from_below, from_above, far_low, far_high


def product(lhs_ref, here, pieces):
    own, below, above, far_low, far_high = pieces
    rows = own.shape[1]
    half = rows // 2
    total = None
    for step, refs in ((0, (own,)), (3, (below,)), (1, (above,)), (2, (far_low, far_high))):
        start = lax.rem(here + step, 4) * rows
        for k, ref in enumerate(refs):
            depth = ref.shape[1]
            columns = pl.ds(pl.multiple_of(start + k * half, half), depth)
            part = jnp.dot(lhs_ref[:, columns], ref[0], preferred_element_type=jnp.float32)
            total = part if total is None else total + part
    return total


def ph_kernel(index, gamma, chi, own, below, above, low, high, base, slots, lhs):
    q = pl.program_id(0)
    g = gamma[0].astype(jnp.float32)
    lhs[...] = (g * chi[0]).astype(jnp.bfloat16)
    phi = product(lhs, index[128], (own, below, above, low, high))
    base[0] = g + phi
    wire = phi.astype(jnp.bfloat16)
    for r in range(RS):
        for c in range(CB):
            slot = index[q * (RS * CB) + r * CB + c]
            slots[slot] = wire[r * 64 : (r + 1) * 64, c * 128 : (c + 1) * 128]


def pp_kernel(index, came, chi, own, below, above, low, high, slots, lhs):
    p = pl.program_id(0)
    for r in range(RS):
        for c in range(CB):
            slot = index[p * (RS * CB) + r * CB + c]
            tile = came[slot].astype(jnp.float32) * chi[0, :, c * 128 : (c + 1) * 128]
            lhs[r * 64 : (r + 1) * 64, c * 128 : (c + 1) * 128] = tile.astype(jnp.bfloat16)
    phi = product(lhs, index[128], (own, below, above, low, high)).astype(jnp.bfloat16)
    for r in range(RS):
        for c in range(CB):
            slot = index[p * (RS * CB) + r * CB + c]
            slots[slot] = phi[r * 64 : (r + 1) * 64, c * 128 : (c + 1) * 128]


def sum_kernel(index, base, came, out):
    q = pl.program_id(0)
    for r in range(RS):
        for c in range(CB):
            slot = index[q * (RS * CB) + r * CB + c]
            rows, columns = slice(r * 64, (r + 1) * 64), slice(c * 128, (c + 1) * 128)
            out[0, rows, columns] = (base[0, rows, columns] + came[slot].astype(jnp.float32)).astype(
                jnp.bfloat16
            )


def point_spec(rows, columns):
    return pl.BlockSpec((1, rows, columns), lambda q, index: (q, 0, 0))


def whole_spec(shape):
    return pl.BlockSpec(shape, lambda q, index: (0,) * len(shape))


PIECES = [point_spec(256, 1024)] * 3 + [point_spec(128, 1024)] * 2
TILES = (192, 64, 128)


def call(kernel, index, operands, in_specs, out_specs, out_shape, scratch, flops, moved):
    return pl.pallas_call(
        kernel,
        grid_spec=pltpu.PrefetchScalarGridSpec(
            num_scalar_prefetch=1,
            grid=(4,),
            in_specs=in_specs,
            out_specs=out_specs,
            scratch_shapes=scratch,
        ),
        out_shape=out_shape,
        compiler_params=pltpu.CompilerParams(vmem_limit_bytes=32 * MIB),
        cost_estimate=pl.CostEstimate(flops=flops, bytes_accessed=moved, transcendentals=0),
    )(index, *operands)


def plan(relabel, points, boson_here, block_here):
    nboson = lax.axis_size("boson")
    item_total = points * RS * CB
    own_targets = lax.dynamic_slice(
        relabel, (boson_here * points, block_here * RS, 0), (points, RS, CB)
    ).reshape(item_total)
    shifts = (own_targets // points - boson_here) % nboson
    item_range = jnp.arange(item_total, dtype=jnp.int32)
    target = own_targets % points * (RS * CB) + item_range % (RS * CB)
    earlier = (shifts[None, :] == shifts[:, None]) & (item_range[None, :] < item_range[:, None])
    rank = jnp.sum(earlier.astype(jnp.int32), axis=1)
    send = (boson_here + shifts) % nboson * CAP + rank
    recv = (boson_here - shifts) % nboson * CAP + rank
    recv_at = jnp.sum(
        (target[None, :] == item_range[:, None]).astype(jnp.int32) * recv[None, :], axis=1
    )
    return send, recv_at


def exchange(slots):
    nboson = lax.axis_size("boson")
    tile = slots.shape[1:]
    return lax.all_to_all(
        slots.reshape((nboson, CAP) + tile), "boson", split_axis=0, concat_axis=0, tiled=True
    ).reshape(slots.shape)


def local(gamma_ph, full_ph, chi_ph, pp_vertex, chi_pp, relabel):
    points = gamma_ph.shape[0]
    block_here = lax.axis_index("block")
    send, recv_at = plan(relabel, points, lax.axis_index("boson"), block_here)
    here = jnp.full((8,), block_here, jnp.int32)
    send_index = jnp.concatenate([send, here])
    recv_index = jnp.concatenate([recv_at, here])
    flops = 2 * 4 * 256 * 1024 * 1024
    ph_pieces = block_rows(full_ph)
    pp_held = lax.optimization_barrier((pp_vertex,) + ph_pieces[1:])[0]
    pp_pieces = block_rows(pp_held)
    lhs = pltpu.VMEM((256, 1024), jnp.bfloat16)
    chi_spec = point_spec(1, 1024)
    tiles = jax.ShapeDtypeStruct(TILES, jnp.bfloat16)
    base, outgoing = call(
        ph_kernel,
        send_index,
        (gamma_ph, chi_ph[:, None, :]) + ph_pieces,
        [point_spec(256, 1024), chi_spec] + PIECES,
        [point_spec(256, 1024), whole_spec(TILES)],
        [jax.ShapeDtypeStruct(gamma_ph.shape, jnp.float32), tiles],
        [lhs],
        flops,
        17 * MIB,
    )
    came = exchange(outgoing)
    leaving = call(
        pp_kernel,
        recv_index,
        (came, chi_pp[:, None, :]) + pp_pieces,
        [whole_spec(TILES), chi_spec] + PIECES,
        whole_spec(TILES),
        tiles,
        [lhs],
        flops,
        14 * MIB,
    )
    back = exchange(leaving)
    return call(
        sum_kernel,
        send_index,
        (base, back),
        [point_spec(256, 1024), whole_spec(TILES)],
        point_spec(256, 1024),
        jax.ShapeDtypeStruct(gamma_ph.shape, jnp.bfloat16),
        [],
        1 * MIB,
        9 * MIB,
    )


def solution(mesh):
    placed = (
        P("boson", "block", None),
        P("boson", "block", None),
        P("boson", None),
        P("boson", "block", None),
        P("boson", None),
        P(),
    )
    return jax.shard_map(
        local, mesh=mesh, in_specs=placed, out_specs=P("boson", "block", None), check_vma=False
    )
```

```python
import jax
import jax.numpy as jnp
from jax import lax
from jax.experimental import pallas as pl
from jax.experimental.pallas import tpu as pltpu
from jax.sharding import PartitionSpec as P

CB = 8
RS = 4
CAP = 3
ITEMS = RS * CB
MIB = 1 << 20
NEAR, FAR = 20, 8
BF16 = jnp.bfloat16
F32 = jnp.float32


def low_lanes(rows):
    return lax.broadcasted_iota(jnp.int32, (rows, 128), 1) < 64


def swap_lanes(x):
    return pltpu.roll(x, 64, 1)


def cut_kernel(high_lanes, x, *outs):
    low = low_lanes(x.shape[1])
    for m in range(4):
        even = x[0, :, m * 256 : m * 256 + 128].astype(F32)
        odd = swap_lanes(x[0, :, m * 256 + 128 : m * 256 + 256].astype(F32))
        lanes = jnp.where(low, odd, even) if high_lanes else jnp.where(low, even, odd)
        out = outs[m * len(outs) // 4]
        to = m * 128 % out.shape[2]
        out[0, :, to : to + 128] = lanes.astype(BF16)


def hold_kernel(x, out):
    pass


def after(value, others):
    return lax.optimization_barrier((value, others))[0]


def gather_rows(parts, between=None):
    n = lax.axis_size("block")
    up = [(i, (i + 1) % n) for i in range(n)]
    down = [(i, (i - 1) % n) for i in range(n)]
    low, high = parts[0], parts[-1]
    below = [lax.ppermute(low, "block", up)]
    above = [lax.ppermute(high, "block", down)]
    if len(parts) == 2:
        below.append(lax.ppermute(high, "block", up))
        above.insert(0, lax.ppermute(low, "block", down))
        near = (below[0], above[1])
    else:
        half = low.shape[2] // 2
        near = (below[0][:, :, :half], above[0][:, :, half:])
    if between is not None:
        near = after(near, between)
    far = [lax.ppermute(near[0], "block", up), lax.ppermute(near[1], "block", down)]
    return tuple(parts) + tuple(below) + tuple(above) + tuple(far)


def product(lhs, here, pieces, half):
    near, far = pieces[:-2], pieces[-2:]
    rows, width = far[0].shape[1:]
    total = None
    for step, part in ((0, near[: len(near) // 3]), (3, near[len(near) // 3 : -len(near) // 3]),
                       (1, near[-len(near) // 3 :]), (2, far)):
        block = part[half][0] if len(part) == 2 else part[0][0, :, half * width : half * width + width]
        start = pl.multiple_of(lax.rem(here + step, 4) * rows, rows)
        term = jnp.dot(lhs[:, pl.ds(start, rows)], block, preferred_element_type=F32)
        total = term if total is None else total + term
    return total


def ph_kernel(odd_ahead, index, gamma, chi, *refs):
    pieces, (phi_out, slots, lhs) = refs[:-3], refs[-3:]
    q = pl.program_id(0)
    lhs[...] = (gamma[0].astype(F32) * chi[0]).astype(BF16)
    low = low_lanes(32)
    for half in range(2):
        phi = product(lhs, index[128], pieces, half)
        phi_out[0, :, half * 256 : half * 256 + 256] = phi
        for r in range(RS):
            for m in range(2):
                pair = phi[r * 64 : r * 64 + 64, m * 128 : m * 128 + 128]
                top, bottom = pair[:32], swap_lanes(pair[32:])
                item = q * ITEMS + r * CB + half * 4 + m * 2
                ahead, behind = (1, 0) if odd_ahead else (0, 1)
                slots[index[item + ahead]] = jnp.where(low, top, bottom).astype(BF16)
                slots[index[item + behind]] = jnp.where(low, bottom, top).astype(BF16)


def pp_kernel(index, first, second, chi, *refs):
    pieces, (slots, lhs) = refs[:-2], refs[-2:]
    p = pl.program_id(0)
    low = low_lanes(32)
    for r in range(RS):
        for c in range(CB):
            slot = index[p * ITEMS + r * CB + c]
            a, b = first[slot].astype(F32), second[slot].astype(F32)
            scale = chi[0, :, c * 128 : c * 128 + 128]
            straight = (jnp.where(low, a, b) * scale).astype(BF16)
            crossed = (swap_lanes(jnp.where(low, b, a)) * scale).astype(BF16)
            top = r * 64 + c % 2 * 32
            other = r * 64 + 32 - c % 2 * 32
            lhs[top : top + 32, c * 128 : c * 128 + 128] = straight
            lhs[other : other + 32, c * 128 : c * 128 + 128] = crossed
    for half in range(2):
        phi = product(lhs, index[128], pieces, half).astype(BF16)
        for r in range(RS):
            for c in range(4):
                slot = index[p * ITEMS + r * CB + half * 4 + c]
                slots[slot] = phi[r * 64 : r * 64 + 64, c * 128 : c * 128 + 128]


def base_kernel(gamma, first, second, out):
    low = low_lanes(256)
    for m in range(4):
        a = first[0, :, m * 128 : m * 128 + 128]
        b = second[0, :, m * 128 : m * 128 + 128]
        for c, phi in ((2 * m, jnp.where(low, a, b)), (2 * m + 1, swap_lanes(jnp.where(low, b, a)))):
            columns = slice(c * 128, c * 128 + 128)
            out[0, :, columns] = gamma[0, :, columns].astype(F32) + phi


def sum_kernel(index, base, came, out):
    q = pl.program_id(0)
    for r in range(RS):
        for c in range(CB):
            rows, columns = slice(r * 64, r * 64 + 64), slice(c * 128, c * 128 + 128)
            back = came[index[q * ITEMS + r * CB + c]].astype(F32)
            out[0, rows, columns] = (base[0, rows, columns] + back).astype(BF16)


def point_spec(rows, columns):
    return pl.BlockSpec((1, rows, columns), lambda q, *index: (q, 0, 0))


def whole_spec(shape):
    return pl.BlockSpec(shape, lambda q, *index: (0,) * len(shape))


def call(
    kernel, index, operands, in_specs, out_specs, out_shape, scratch, us, grant, free=(), **other
):
    return pl.pallas_call(
        kernel,
        grid_spec=pltpu.PrefetchScalarGridSpec(
            num_scalar_prefetch=len(index),
            grid=other.get("grid", (4,)),
            in_specs=in_specs,
            out_specs=out_specs,
            scratch_shapes=scratch,
        ),
        out_shape=out_shape,
        compiler_params=pltpu.CompilerParams(vmem_limit_bytes=grant * MIB),
        cost_estimate=pl.CostEstimate(
            flops=int(us * 1e9), bytes_accessed=int(us * 3e6), transcendentals=0
        ),
        input_output_aliases=other.get("aliases", {}),
    )(
        *index,
        *(
            x if k in free else pltpu.with_memory_space_constraint(x, pltpu.HBM)
            for k, x in enumerate(operands)
        ),
    )


def plan(relabel, points, boson_here, block_here):
    nboson = lax.axis_size("boson")
    item_total = points * ITEMS
    own_targets = lax.dynamic_slice(
        relabel, (boson_here * points, block_here * RS, 0), (points, RS, CB)
    ).reshape(item_total)
    shifts = (own_targets // points - boson_here) % nboson
    item_range = jnp.arange(item_total, dtype=jnp.int32)
    target = own_targets % points * ITEMS + item_range % ITEMS
    earlier = (shifts[None, :] == shifts[:, None]) & (item_range[None, :] < item_range[:, None])
    rank = jnp.sum(earlier.astype(jnp.int32), axis=1)
    send = (boson_here + shifts) % nboson * CAP + rank
    recv = (boson_here - shifts) % nboson * CAP + rank
    recv_at = jnp.sum(
        (target[None, :] == item_range[:, None]).astype(jnp.int32) * recv[None, :], axis=1
    )
    return send, recv_at


def exchange(slots):
    nboson = lax.axis_size("boson")
    tile = slots.shape[1:]
    return lax.all_to_all(
        slots.reshape((nboson, CAP) + tile), "boson", split_axis=0, concat_axis=0, tiled=True
    ).reshape(slots.shape)


def local(gamma_ph, full_ph, chi_ph, pp_vertex, chi_pp, relabel):
    block_here = lax.axis_index("block")
    send, recv_at = plan(relabel, gamma_ph.shape[0], lax.axis_index("boson"), block_here)
    here = jnp.full((8,), block_here, jnp.int32)
    send_index = jnp.concatenate([send, here])
    recv_index = jnp.concatenate([recv_at, here])

    half_tiles = pltpu.HBM((64 * CAP, 32, 128), BF16)
    tiles = pltpu.HBM((64 * CAP, 64, 128), BF16)
    lhs = pltpu.VMEM((256, 1024), BF16)
    row_spec, chi_spec = point_spec(256, 1024), point_spec(1, 1024)

    def specs(pieces):
        return [point_spec(*x.shape[1:]) for x in pieces]

    def cut(high_lanes, parts):
        def kernel(*refs):
            cut_kernel(high_lanes, *refs)

        width = 512 // parts
        return call(
            kernel,
            (),
            (full_ph,),
            [row_spec],
            [point_spec(256, width)] * parts,
            [pltpu.HBM((4, 256, width), BF16)] * parts,
            [],
            2,
            6,
        )

    def hold(x, us):
        anywhere = pl.BlockSpec(memory_space=pl.ANY)
        out = pltpu.HBM(x.shape, x.dtype)
        return call(
            hold_kernel, (), (x,), [anywhere], anywhere, out, [], us, 1, grid=(1,), aliases={0: 0}
        )

    def ph_half(odd_ahead, pieces, us):
        def kernel(*refs):
            ph_kernel(odd_ahead, *refs)

        return call(
            kernel,
            (send_index,),
            (gamma_ph, chi_ph[:, None, :]) + pieces,
            [row_spec, chi_spec] + specs(pieces),
            [point_spec(256, 512), whole_spec(half_tiles.inner_aval.shape)],
            [pltpu.HBM((4, 256, 512), F32), half_tiles],
            [lhs],
            us,
            14,
            free=(len(pieces), len(pieces) + 1),
        )

    pieces_1 = gather_rows(cut(False, 2))
    phi_1, outgoing_1 = ph_half(False, pieces_1, 4)
    pieces_2 = gather_rows(after(cut(True, 1), pieces_1), between=outgoing_1)
    came_1 = exchange(outgoing_1)
    phi_2, outgoing_2 = ph_half(True, pieces_2, NEAR)
    pp_pieces = gather_rows((after(pp_vertex, pieces_2),), between=outgoing_2)
    came_2 = exchange(outgoing_2)
    pp_pieces = (pp_pieces[0],) + tuple(hold(x, FAR) for x in pp_pieces[1:3]) + pp_pieces[3:]
    leaving = call(
        pp_kernel,
        (recv_index,),
        (came_1, came_2, chi_pp[:, None, :]) + pp_pieces,
        [whole_spec(half_tiles.inner_aval.shape)] * 2 + [chi_spec] + specs(pp_pieces),
        whole_spec(tiles.inner_aval.shape),
        tiles,
        [lhs],
        5,
        22,
        free=(1, len(pp_pieces) + 1, len(pp_pieces) + 2),
    )
    phi_specs = [point_spec(256, 512)] * 2
    base = call(
        base_kernel,
        (),
        (gamma_ph, phi_1, phi_2),
        [row_spec] + phi_specs,
        row_spec,
        pltpu.HBM(gamma_ph.shape, F32),
        [],
        4,
        10,
    )
    back = exchange(leaving)
    return call(
        sum_kernel,
        (send_index,),
        (base, back),
        [row_spec, whole_spec(tiles.inner_aval.shape)],
        row_spec,
        pltpu.HBM(gamma_ph.shape, BF16),
        [],
        3,
        14,
        free=(1,),
    )


def solution(mesh):
    placed = (
        P("boson", "block", None),
        P("boson", "block", None),
        P("boson", None),
        P("boson", "block", None),
        P("boson", None),
        P(),
    )
    return jax.shard_map(
        local, mesh=mesh, in_specs=placed, out_specs=P("boson", "block", None), check_vma=False
    )
```

```python
import jax
import jax.numpy as jnp
from jax import lax
from jax.experimental import pallas as pl
from jax.experimental.pallas import tpu as pltpu
from jax.sharding import PartitionSpec as P

CB = 8
RS = 4
CAP = 3
ITEMS = RS * CB
MIB = 1 << 20
NEAR, FAR = 20, 8
BF16 = jnp.bfloat16
F32 = jnp.float32


def low_lanes(rows):
    return lax.broadcasted_iota(jnp.int32, (rows, 128), 1) < 64


def swap_lanes(x):
    return pltpu.roll(x, 64, 1)


def start_all(copies):
    for copy in copies:
        copy.start()
    return copies


def wait_all(copies):
    for copy in copies:
        copy.wait()


def point_loads(sources, targets, sems):
    return [
        start_all(
            [
                pltpu.make_async_copy(x.at[q], y.at[q], sems.at[k, q])
                for k, (x, y) in enumerate(zip(sources, targets))
            ]
        )
        for q in range(4)
    ]


def right_loads(pieces, block_here, right, sems):
    split = len(pieces) == 8
    width = pieces[0].shape[2]
    if split:
        where = [(step, 0, half * width) for step in (0, 3, 1, 2) for half in range(2)]
    else:
        where = [(0, 0, 0), (3, 0, 0), (1, 0, 0), (2, 0, 0), (2, 128, 0)]
    loads = []
    for q in range(4):
        copies = []
        for k, (piece, (step, offset, column)) in enumerate(zip(pieces, where)):
            start = pl.multiple_of(lax.rem(block_here + step, 4) * 256 + offset, 128)
            to = right.at[q, pl.ds(start, piece.shape[1]), column : column + width]
            copies.append(pltpu.make_async_copy(piece.at[q], to, sems.at[k, q]))
        loads.append(start_all(copies))
    return loads


def cut_kernel(high_lanes, x, *refs):
    n = (len(refs) - 3) // 2
    outs, x_here, outs_here, in_sems, out_sems = refs[:n], refs[n], refs[n + 1 : -2], refs[-2], refs[-1]
    loads = point_loads([x], [x_here], in_sems)
    low = low_lanes(256)
    stores = []
    for q in range(4):
        wait_all(loads[q])
        for m in range(4):
            even = x_here[q, :, m * 256 : m * 256 + 128].astype(F32)
            odd = swap_lanes(x_here[q, :, m * 256 + 128 : m * 256 + 256].astype(F32))
            lanes = jnp.where(low, odd, even) if high_lanes else jnp.where(low, even, odd)
            out = outs_here[m * n // 4]
            to = m * 128 % out.shape[2]
            out[q, :, to : to + 128] = lanes.astype(BF16)
        stores += start_all(
            [
                pltpu.make_async_copy(y.at[q], out.at[q], out_sems.at[k, q])
                for k, (y, out) in enumerate(zip(outs_here, outs))
            ]
        )
    wait_all(stores)


def hold_kernel(x, out):
    pass


def after(value, others):
    return lax.optimization_barrier((value, others))[0]


def gather_rows(parts, between=None):
    n = lax.axis_size("block")
    up = [(i, (i + 1) % n) for i in range(n)]
    down = [(i, (i - 1) % n) for i in range(n)]
    low, high = parts[0], parts[-1]
    below = [lax.ppermute(low, "block", up)]
    above = [lax.ppermute(high, "block", down)]
    if len(parts) == 2:
        below.append(lax.ppermute(high, "block", up))
        above.insert(0, lax.ppermute(low, "block", down))
        near = (below[0], above[1])
    else:
        half = low.shape[1] // 2
        near = (below[0][:, :half], above[0][:, half:])
    if between is not None:
        near = after(near, between)
    far = [lax.ppermute(near[0], "block", up), lax.ppermute(near[1], "block", down)]
    return tuple(parts) + tuple(below) + tuple(above) + tuple(far)


def scale_kernel(gamma, chi, out):
    row = chi[pl.ds(pl.program_id(0), 1), :]
    out[0] = (gamma[0].astype(F32) * row).astype(BF16)


def ph_kernel(odd_ahead, n, index, scaled, *refs):
    pieces, (phi_out, slots_out) = refs[:n], refs[n : n + 2]
    left, right, phi, slots, left_sems, in_sems, out_sems = refs[n + 2 :]
    left_loads = point_loads([scaled], [left], left_sems)
    loads = right_loads(pieces, index[128], right, in_sems)
    low = low_lanes(32)
    stores = []
    for q in range(4):
        wait_all(left_loads[q] + loads[q])
        for half in range(2):
            columns = slice(half * 256, half * 256 + 256)
            part = jnp.dot(left[q], right[q, :, columns], preferred_element_type=F32)
            phi[q, :, columns] = part
            for r in range(RS):
                for m in range(2):
                    pair = part[r * 64 : r * 64 + 64, m * 128 : m * 128 + 128]
                    top, bottom = pair[:32], swap_lanes(pair[32:])
                    item = q * ITEMS + r * CB + half * 4 + m * 2
                    ahead, behind = (1, 0) if odd_ahead else (0, 1)
                    slots[index[item + ahead]] = jnp.where(low, top, bottom).astype(BF16)
                    slots[index[item + behind]] = jnp.where(low, bottom, top).astype(BF16)
        stores += start_all([pltpu.make_async_copy(phi.at[q], phi_out.at[q], out_sems.at[q])])
    stores += start_all([pltpu.make_async_copy(slots, slots_out, out_sems.at[4])])
    wait_all(stores)


def pp_kernel(n, index, first_in, second_in, chi, *refs):
    pieces, slots_out = refs[:n], refs[n]
    right, first, second, slots, lhs, in_sems, slot_sems = refs[n + 1 :]
    arrivals = start_all(
        [
            pltpu.make_async_copy(first_in, first, slot_sems.at[0]),
            pltpu.make_async_copy(second_in, second, slot_sems.at[1]),
        ]
    )
    loads = right_loads(pieces, index[128], right, in_sems)
    wait_all(arrivals)
    low = low_lanes(32)
    for p in range(4):
        row = chi[p : p + 1, :]
        for r in range(RS):
            for c in range(CB):
                slot = index[p * ITEMS + r * CB + c]
                a, b = first[slot].astype(F32), second[slot].astype(F32)
                scale = row[:, c * 128 : c * 128 + 128]
                straight = (jnp.where(low, a, b) * scale).astype(BF16)
                crossed = (swap_lanes(jnp.where(low, b, a)) * scale).astype(BF16)
                top = r * 64 + c % 2 * 32
                other = r * 64 + 32 - c % 2 * 32
                lhs[top : top + 32, c * 128 : c * 128 + 128] = straight
                lhs[other : other + 32, c * 128 : c * 128 + 128] = crossed
        wait_all(loads[p])
        for half in range(2):
            columns = slice(half * 512, half * 512 + 512)
            phi = jnp.dot(lhs[...], right[p, :, columns], preferred_element_type=F32).astype(BF16)
            for r in range(RS):
                for c in range(4):
                    slot = index[p * ITEMS + r * CB + half * 4 + c]
                    slots[slot] = phi[r * 64 : r * 64 + 64, c * 128 : c * 128 + 128]
    wait_all(start_all([pltpu.make_async_copy(slots, slots_out, slot_sems.at[2])]))


def base_kernel(gamma, first, second, out):
    low = low_lanes(256)
    for m in range(4):
        a = first[0, :, m * 128 : m * 128 + 128]
        b = second[0, :, m * 128 : m * 128 + 128]
        for c, phi in ((2 * m, jnp.where(low, a, b)), (2 * m + 1, swap_lanes(jnp.where(low, b, a)))):
            columns = slice(c * 128, c * 128 + 128)
            out[0, :, columns] = gamma[0, :, columns].astype(F32) + phi


def sum_kernel(index, base_in, came_in, out, base, came, total, in_sems, out_sems):
    arrival = start_all([pltpu.make_async_copy(came_in, came, out_sems.at[4])])
    loads = point_loads([base_in], [base], in_sems)
    wait_all(arrival)
    stores = []
    for q in range(4):
        wait_all(loads[q])
        for r in range(RS):
            for c in range(CB):
                rows, columns = slice(r * 64, r * 64 + 64), slice(c * 128, c * 128 + 128)
                back = came[index[q * ITEMS + r * CB + c]].astype(F32)
                total[q, rows, columns] = (base[q, rows, columns] + back).astype(BF16)
        stores += start_all([pltpu.make_async_copy(total.at[q], out.at[q], out_sems.at[q])])
    wait_all(stores)


def point_spec(rows, columns):
    return pl.BlockSpec((1, rows, columns), lambda q, *index: (q, 0, 0))


def whole_spec(shape):
    return pl.BlockSpec(shape, lambda q, *index: (0,) * len(shape))


def call(
    kernel, index, operands, in_specs, out_specs, out_shape, scratch, us, grant, free=(), **other
):
    return pl.pallas_call(
        kernel,
        grid_spec=pltpu.PrefetchScalarGridSpec(
            num_scalar_prefetch=len(index),
            grid=other.get("grid", (4,)),
            in_specs=in_specs,
            out_specs=out_specs,
            scratch_shapes=scratch,
        ),
        out_shape=out_shape,
        compiler_params=pltpu.CompilerParams(vmem_limit_bytes=grant * MIB),
        cost_estimate=pl.CostEstimate(
            flops=int(us * 1e9), bytes_accessed=int(us * 3e6), transcendentals=0
        ),
        input_output_aliases=other.get("aliases", {}),
    )(
        *index,
        *(
            x if k in free else pltpu.with_memory_space_constraint(x, pltpu.HBM)
            for k, x in enumerate(operands)
        ),
    )


def plan(relabel, points, boson_here, block_here):
    nboson = lax.axis_size("boson")
    item_total = points * ITEMS
    own_targets = lax.dynamic_slice(
        relabel, (boson_here * points, block_here * RS, 0), (points, RS, CB)
    ).reshape(item_total)
    shifts = (own_targets // points - boson_here) % nboson
    item_range = jnp.arange(item_total, dtype=jnp.int32)
    target = own_targets % points * ITEMS + item_range % ITEMS
    earlier = (shifts[None, :] == shifts[:, None]) & (item_range[None, :] < item_range[:, None])
    rank = jnp.sum(earlier.astype(jnp.int32), axis=1)
    send = (boson_here + shifts) % nboson * CAP + rank
    recv = (boson_here - shifts) % nboson * CAP + rank
    recv_at = jnp.sum(
        (target[None, :] == item_range[:, None]).astype(jnp.int32) * recv[None, :], axis=1
    )
    return send, recv_at


def exchange(slots):
    nboson = lax.axis_size("boson")
    tile = slots.shape[1:]
    return lax.all_to_all(
        slots.reshape((nboson, CAP) + tile), "boson", split_axis=0, concat_axis=0, tiled=True
    ).reshape(slots.shape)


HALF_TILES = (64 * CAP, 32, 128)
TILES = (64 * CAP, 64, 128)
ROWS = point_spec(256, 1024)
CHI = whole_spec((4, 1024))


def specs(pieces):
    return [point_spec(*x.shape[1:]) for x in pieces]


ANY = pl.BlockSpec(memory_space=pl.ANY)
DMA = pltpu.SemaphoreType.DMA


def vmem(x):
    return pltpu.VMEM(x.shape, x.dtype)


def cut(full, high_lanes, parts):
    def kernel(*refs):
        cut_kernel(high_lanes, *refs)

    shape = (4, 256, 512 // parts)
    scratch = [vmem(full)] + [pltpu.VMEM(shape, BF16)] * parts + [DMA((1, 4)), DMA((parts, 4))]
    outs = [jax.ShapeDtypeStruct(shape, BF16)] * parts
    return call(kernel, (), (full,), [ANY], [ANY] * parts, outs, scratch, 2, 6, grid=())


def scale_rows(gamma, chi):
    out = jax.ShapeDtypeStruct(gamma.shape, BF16)
    return call(scale_kernel, (), (gamma, chi), [ROWS, CHI], ROWS, out, [], 2, 6)


def hold(x, us):
    anywhere = pl.BlockSpec(memory_space=pl.ANY)
    out = pltpu.HBM(x.shape, x.dtype)
    return call(
        hold_kernel, (), (x,), [anywhere], anywhere, out, [], us, 1, grid=(1,), aliases={0: 0}
    )


def ph_half(odd_ahead, index, scaled, pieces, us):
    n = len(pieces)

    def kernel(*refs):
        ph_kernel(odd_ahead, n, *refs)

    phi = (4, 256, 512)
    scratch = [vmem(scaled), pltpu.VMEM((4, 1024, 512), BF16), pltpu.VMEM(phi, F32)]
    scratch += [pltpu.VMEM(HALF_TILES, BF16), DMA((1, 4)), DMA((n, 4)), DMA((5,))]
    outs = [pltpu.HBM(phi, F32), pltpu.HBM(HALF_TILES, BF16)]
    return call(
        kernel,
        (index,),
        (scaled,) + pieces,
        [ANY] * (n + 1),
        [ANY] * 2,
        outs,
        scratch,
        us,
        14,
        free=tuple(range(n + 1)) if n == 8 else (),
        grid=(),
    )


def pp_whole(index, came_1, came_2, chi, pieces):
    n = len(pieces)

    def kernel(*refs):
        pp_kernel(n, *refs)

    scratch = [pltpu.VMEM((4, 1024, 1024), BF16), vmem(came_1), vmem(came_2)]
    scratch += [pltpu.VMEM(TILES, BF16), pltpu.VMEM((256, 1024), BF16), DMA((n, 4)), DMA((3,))]
    return call(
        kernel,
        (index,),
        (came_1, came_2, chi) + pieces,
        [ANY, ANY, pl.BlockSpec(memory_space=pltpu.VMEM)] + [ANY] * n,
        ANY,
        pltpu.HBM(TILES, BF16),
        scratch,
        5,
        22,
        free=(1, n + 1, n + 2),
        grid=(),
    )


def base_sum(gamma, phi_1, phi_2):
    return call(
        base_kernel,
        (),
        (gamma, phi_1, phi_2),
        [ROWS] + [point_spec(256, 512)] * 2,
        ROWS,
        pltpu.HBM(gamma.shape, F32),
        [],
        4,
        10,
    )


def last_sum(index, base, back):
    out = pltpu.HBM(base.shape, BF16)
    scratch = [vmem(base), vmem(back), pltpu.VMEM(base.shape, BF16), DMA((1, 4)), DMA((5,))]
    return call(
        sum_kernel, (index,), (base, back), [ANY] * 2, ANY, out, scratch, 3, 14, free=(1,), grid=()
    )


def local(gamma_ph, full_ph, chi_ph, pp_vertex, chi_pp, relabel):
    block_here = lax.axis_index("block")
    send, recv_at = plan(relabel, gamma_ph.shape[0], lax.axis_index("boson"), block_here)
    here = jnp.full((8,), block_here, jnp.int32)
    send_index = jnp.concatenate([send, here])
    recv_index = jnp.concatenate([recv_at, here])

    full_ph, gamma_ph = after((full_ph, gamma_ph), (send_index, recv_index))
    scaled = scale_rows(gamma_ph, chi_ph)
    pieces_1 = gather_rows(cut(full_ph, False, 2))
    phi_1, outgoing_1 = ph_half(False, send_index, scaled, pieces_1, 4)
    pieces_2 = gather_rows(after(cut(full_ph, True, 1), pieces_1), between=outgoing_1)
    came_1 = exchange(outgoing_1)
    phi_2, outgoing_2 = ph_half(True, send_index, scaled, pieces_2, NEAR)
    pp_pieces = gather_rows((after(pp_vertex, pieces_2),), between=outgoing_2)
    came_2 = exchange(outgoing_2)
    pp_pieces = (pp_pieces[0],) + tuple(hold(x, FAR) for x in pp_pieces[1:3]) + pp_pieces[3:]
    leaving = pp_whole(recv_index, came_1, came_2, chi_pp, pp_pieces)
    base = base_sum(gamma_ph, phi_1, phi_2)
    return last_sum(send_index, base, exchange(leaving))


def solution(mesh):
    placed = (
        P("boson", "block", None),
        P("boson", "block", None),
        P("boson", None),
        P("boson", "block", None),
        P("boson", None),
        P(),
    )
    return jax.shard_map(
        local, mesh=mesh, in_specs=placed, out_specs=P("boson", "block", None), check_vma=False
    )
```

```python
import jax
import jax.numpy as jnp
from jax import lax
from jax.experimental import pallas as pl
from jax.experimental.pallas import tpu as pltpu
from jax.sharding import PartitionSpec as P

CB = 8
RS = 4
CAP = 3
ITEMS = RS * CB
MIB = 1 << 20
NEAR, FAR = 20, 8
BF16 = jnp.bfloat16
F32 = jnp.float32


def low_lanes(rows):
    return lax.broadcasted_iota(jnp.int32, (rows, 128), 1) < 64


def swap_lanes(x):
    return pltpu.roll(x, 64, 1)


def start_all(copies):
    for copy in copies:
        copy.start()
    return copies


def wait_all(copies):
    for copy in copies:
        copy.wait()


def point_loads(sources, targets, sems):
    return [
        start_all(
            [
                pltpu.make_async_copy(x.at[q], y.at[q], sems.at[k, q])
                for k, (x, y) in enumerate(zip(sources, targets))
            ]
        )
        for q in range(4)
    ]


def right_loads(pieces, block_here, right, sems):
    where = [(step, offset) for step in STEPS for offset in (0, 128)]
    where = [(s, o) for k, (s, o) in enumerate(where) if len(pieces) == 8 or o == 0 or k == 7]
    loads = []
    for q in range(4):
        copies = []
        for k, (piece, (step, offset)) in enumerate(zip(pieces, where)):
            start = pl.multiple_of(lax.rem(block_here + step, 4) * 256 + offset, 128)
            to = right.at[q, pl.ds(start, piece.shape[1])]
            copies.append(pltpu.make_async_copy(piece.at[q], to, sems.at[k, q]))
        loads.append(start_all(copies))
    return loads


def cut_kernel(high_lanes, x, *refs):
    n = (len(refs) - 3) // 2
    outs, x_here, outs_here, in_sems, out_sems = refs[:n], refs[n], refs[n + 1 : -2], refs[-2], refs[-1]
    loads = point_loads([x], [x_here], in_sems)
    low = low_lanes(256)
    stores = []
    for q in range(4):
        wait_all(loads[q])
        for m in range(4):
            even = x_here[q, :, m * 256 : m * 256 + 128].astype(F32)
            odd = swap_lanes(x_here[q, :, m * 256 + 128 : m * 256 + 256].astype(F32))
            lanes = jnp.where(low, odd, even) if high_lanes else jnp.where(low, even, odd)
            out = outs_here[m * n // 4]
            to = m * 128 % out.shape[2]
            out[q, :, to : to + 128] = lanes.astype(BF16)
        stores += start_all(
            [
                pltpu.make_async_copy(y.at[q], out.at[q], out_sems.at[k, q])
                for k, (y, out) in enumerate(zip(outs_here, outs))
            ]
        )
    wait_all(stores)


def hold_kernel(x, out):
    pass


def after(value, others):
    return lax.optimization_barrier((value, others))[0]


def gather_rows(low, high, between=None):
    n = lax.axis_size("block")
    up = [(i, (i + 1) % n) for i in range(n)]
    down = [(i, (i - 1) % n) for i in range(n)]
    below_low = lax.ppermute(low, "block", up)
    above_high = lax.ppermute(high, "block", down)
    below_high = lax.ppermute(high, "block", up)
    above_low = lax.ppermute(low, "block", down)
    near = (below_low, above_high)
    if between is not None:
        near = after(near, between)
    far_low = lax.ppermute(near[0], "block", up)
    far_high = lax.ppermute(near[1], "block", down)
    return low, high, below_low, below_high, above_low, above_high, far_low, far_high


def gather_whole(own, between):
    n = lax.axis_size("block")
    up = [(i, (i + 1) % n) for i in range(n)]
    down = [(i, (i - 1) % n) for i in range(n)]
    half = own.shape[1] // 2
    below = lax.ppermute(own, "block", up)
    above = lax.ppermute(own, "block", down)
    near_low, near_high = after((below[:, :half], above[:, half:]), between)
    return (
        own,
        below,
        above,
        lax.ppermute(near_low, "block", up),
        lax.ppermute(near_high, "block", down),
    )


STEPS = (0, 3, 1, 2)


def product(lhs, here, pieces, q, half):
    total = None
    for k, step in enumerate(STEPS):
        start = pl.multiple_of(lax.rem(here + step, 4) * 256, 256)
        block = pieces[2 * k + half][q]
        term = jnp.dot(lhs[:, pl.ds(start, 256)], block, preferred_element_type=F32)
        total = term if total is None else total + term
    return total


def scale_kernel(gamma, chi, out):
    row = chi[pl.ds(pl.program_id(0), 1), :]
    out[0] = (gamma[0].astype(F32) * row).astype(BF16)


def ph_kernel(second, index, scaled, *refs):
    n = 5 if second else 8
    pieces, (phi_out, slots_out, phi, slots, out_sems) = refs[:n], refs[n : n + 5]
    if second:
        left, right, left_sems, in_sems = refs[n + 5 :]
        left_loads = point_loads([scaled], [left], left_sems)
        loads = right_loads(pieces, index[128], right, in_sems)
    low = low_lanes(32)
    stores = []
    for q in range(4):
        if second:
            wait_all(left_loads[q] + loads[q])
        for half in range(2):
            columns = slice(half * 256, half * 256 + 256)
            if second:
                part = jnp.dot(left[q], right[q, :, columns], preferred_element_type=F32)
            else:
                part = product(scaled.at[q], index[128], pieces, q, half)
            phi[q, :, columns] = part
            for r in range(RS):
                for m in range(2):
                    pair = part[r * 64 : r * 64 + 64, m * 128 : m * 128 + 128]
                    top, bottom = pair[:32], swap_lanes(pair[32:])
                    item = q * ITEMS + r * CB + half * 4 + m * 2
                    ahead, behind = (1, 0) if second else (0, 1)
                    slots[index[item + ahead]] = jnp.where(low, top, bottom).astype(BF16)
                    slots[index[item + behind]] = jnp.where(low, bottom, top).astype(BF16)
        stores += start_all([pltpu.make_async_copy(phi.at[q], phi_out.at[q], out_sems.at[q])])
    stores += start_all([pltpu.make_async_copy(slots, slots_out, out_sems.at[4])])
    wait_all(stores)


def pp_kernel(index, first_in, second, chi, *refs):
    pieces, slots_out = refs[:8], refs[8]
    right, first, slots, lhs, in_sems, slot_sems = refs[9:]
    arrivals = start_all([pltpu.make_async_copy(first_in, first, slot_sems.at[0])])
    loads = right_loads(pieces, index[128], right, in_sems)
    wait_all(arrivals)
    low = low_lanes(32)
    for p in range(4):
        row = chi[p : p + 1, :]
        for r in range(RS):
            for c in range(CB):
                slot = index[p * ITEMS + r * CB + c]
                a, b = first[slot].astype(F32), second[slot].astype(F32)
                scale = row[:, c * 128 : c * 128 + 128]
                straight = (jnp.where(low, a, b) * scale).astype(BF16)
                crossed = (swap_lanes(jnp.where(low, b, a)) * scale).astype(BF16)
                top = r * 64 + c % 2 * 32
                other = r * 64 + 32 - c % 2 * 32
                lhs[top : top + 32, c * 128 : c * 128 + 128] = straight
                lhs[other : other + 32, c * 128 : c * 128 + 128] = crossed
        wait_all(loads[p])
        for half in range(2):
            columns = slice(half * 512, half * 512 + 512)
            phi = jnp.dot(lhs[...], right[p, :, columns], preferred_element_type=F32).astype(BF16)
            for r in range(RS):
                for c in range(4):
                    slot = index[p * ITEMS + r * CB + half * 4 + c]
                    slots[slot] = phi[r * 64 : r * 64 + 64, c * 128 : c * 128 + 128]
    wait_all(start_all([pltpu.make_async_copy(slots, slots_out, slot_sems.at[1])]))


def base_kernel(gamma, first, second, out):
    low = low_lanes(256)
    for m in range(4):
        a = first[0, :, m * 128 : m * 128 + 128]
        b = second[0, :, m * 128 : m * 128 + 128]
        for c, phi in ((2 * m, jnp.where(low, a, b)), (2 * m + 1, swap_lanes(jnp.where(low, b, a)))):
            columns = slice(c * 128, c * 128 + 128)
            out[0, :, columns] = gamma[0, :, columns].astype(F32) + phi


def sum_kernel(index, base_in, came, out, base, total, in_sems, out_sems):
    loads = point_loads([base_in], [base], in_sems)
    stores = []
    for q in range(4):
        wait_all(loads[q])
        for r in range(RS):
            for c in range(CB):
                rows, columns = slice(r * 64, r * 64 + 64), slice(c * 128, c * 128 + 128)
                back = came[index[q * ITEMS + r * CB + c]].astype(F32)
                total[q, rows, columns] = (base[q, rows, columns] + back).astype(BF16)
        stores += start_all([pltpu.make_async_copy(total.at[q], out.at[q], out_sems.at[q])])
    wait_all(stores)


def point_spec(rows, columns):
    return pl.BlockSpec((1, rows, columns), lambda q, *index: (q, 0, 0))


def whole_spec(shape):
    return pl.BlockSpec(shape, lambda q, *index: (0,) * len(shape))


def call(
    kernel, index, operands, in_specs, out_specs, out_shape, scratch, us, grant, free=(), **other
):
    return pl.pallas_call(
        kernel,
        grid_spec=pltpu.PrefetchScalarGridSpec(
            num_scalar_prefetch=len(index),
            grid=other.get("grid", (4,)),
            in_specs=in_specs,
            out_specs=out_specs,
            scratch_shapes=scratch,
        ),
        out_shape=out_shape,
        compiler_params=pltpu.CompilerParams(vmem_limit_bytes=grant * MIB),
        cost_estimate=pl.CostEstimate(
            flops=int(us * 1e9), bytes_accessed=int(us * 3e6), transcendentals=0
        ),
        input_output_aliases=other.get("aliases", {}),
    )(
        *index,
        *(
            x if k in free else pltpu.with_memory_space_constraint(x, pltpu.HBM)
            for k, x in enumerate(operands)
        ),
    )


def plan(relabel, points, boson_here, block_here):
    nboson = lax.axis_size("boson")
    item_total = points * ITEMS
    own_targets = lax.dynamic_slice(
        relabel, (boson_here * points, block_here * RS, 0), (points, RS, CB)
    ).reshape(item_total)
    shifts = (own_targets // points - boson_here) % nboson
    item_range = jnp.arange(item_total, dtype=jnp.int32)
    target = own_targets % points * ITEMS + item_range % ITEMS
    earlier = (shifts[None, :] == shifts[:, None]) & (item_range[None, :] < item_range[:, None])
    rank = jnp.sum(earlier.astype(jnp.int32), axis=1)
    send = (boson_here + shifts) % nboson * CAP + rank
    recv = (boson_here - shifts) % nboson * CAP + rank
    recv_at = jnp.sum(
        (target[None, :] == item_range[:, None]).astype(jnp.int32) * recv[None, :], axis=1
    )
    return send, recv_at


def exchange(slots):
    nboson = lax.axis_size("boson")
    tile = slots.shape[1:]
    return lax.all_to_all(
        slots.reshape((nboson, CAP) + tile), "boson", split_axis=0, concat_axis=0, tiled=True
    ).reshape(slots.shape)


HALF_TILES = (64 * CAP, 32, 128)
TILES = (64 * CAP, 64, 128)
ROWS = point_spec(256, 1024)
CHI = whole_spec((4, 1024))


def specs(pieces):
    return [point_spec(*x.shape[1:]) for x in pieces]


ANY = pl.BlockSpec(memory_space=pl.ANY)
NEAR_BY = pl.BlockSpec(memory_space=pltpu.VMEM)
DMA = pltpu.SemaphoreType.DMA


def vmem(x):
    return pltpu.VMEM(x.shape, x.dtype)


def cut(full, high_lanes):
    def kernel(*refs):
        cut_kernel(high_lanes, *refs)

    parts = 1 if high_lanes else 2
    shape = (4, 256, 512 // parts)
    scratch = [vmem(full)] + [pltpu.VMEM(shape, BF16)] * parts + [DMA((1, 4)), DMA((parts, 4))]
    outs = [jax.ShapeDtypeStruct(shape, BF16)] * parts
    return call(kernel, (), (full,), [ANY], [ANY] * parts, outs, scratch, 2, 6, grid=())


def scale_rows(gamma, chi):
    out = jax.ShapeDtypeStruct(gamma.shape, BF16)
    return call(scale_kernel, (), (gamma, chi), [ROWS, CHI], ROWS, out, [], 2, 6)


def hold(x, us):
    anywhere = pl.BlockSpec(memory_space=pl.ANY)
    out = pltpu.HBM(x.shape, x.dtype)
    return call(
        hold_kernel, (), (x,), [anywhere], anywhere, out, [], us, 1, grid=(1,), aliases={0: 0}
    )


def ph_half(second, index, scaled, pieces, us):
    def kernel(*refs):
        ph_kernel(second, *refs)

    phi = (4, 256, 512)
    scratch = [pltpu.VMEM(phi, F32), pltpu.VMEM(HALF_TILES, BF16), DMA((5,))]
    if second:
        scratch += [vmem(scaled), pltpu.VMEM((4, 1024, 512), BF16), DMA((1, 4)), DMA((5, 4))]
    return call(
        kernel,
        (index,),
        (scaled,) + pieces,
        [ANY if second else NEAR_BY] * (len(pieces) + 1),
        [ANY] * 2,
        [pltpu.HBM(phi, F32), pltpu.HBM(HALF_TILES, BF16)],
        scratch,
        us,
        14 if second else 8,
        free=() if second else tuple(range(9)),
        grid=(),
    )


def pp_whole(index, came_1, came_2, chi, pieces):
    scratch = [pltpu.VMEM((4, 1024, 1024), BF16), vmem(came_1), pltpu.VMEM(TILES, BF16)]
    scratch += [pltpu.VMEM((256, 1024), BF16), DMA((8, 4)), DMA((2,))]
    return call(
        pp_kernel,
        (index,),
        (came_1, came_2, chi) + pieces,
        [ANY, NEAR_BY, NEAR_BY] + [ANY] * 8,
        ANY,
        pltpu.HBM(TILES, BF16),
        scratch,
        5,
        20,
        free=(1, 2, 9, 10),
        grid=(),
    )


def base_sum(gamma, phi_1, phi_2):
    return call(
        base_kernel,
        (),
        (gamma, phi_1, phi_2),
        [ROWS] + [point_spec(256, 512)] * 2,
        ROWS,
        pltpu.HBM(gamma.shape, F32),
        [],
        4,
        10,
    )


def last_sum(index, base, back):
    out = pltpu.HBM(base.shape, BF16)
    scratch = [vmem(base), pltpu.VMEM(base.shape, BF16), DMA((1, 4)), DMA((4,))]
    return call(
        sum_kernel,
        (index,),
        (base, back),
        [ANY, NEAR_BY],
        ANY,
        out,
        scratch,
        3,
        10,
        free=(1,),
        grid=(),
    )


def local(gamma_ph, full_ph, chi_ph, pp_vertex, chi_pp, relabel):
    block_here = lax.axis_index("block")
    send, recv_at = plan(relabel, gamma_ph.shape[0], lax.axis_index("boson"), block_here)
    here = jnp.full((8,), block_here, jnp.int32)
    send_index = jnp.concatenate([send, here])
    recv_index = jnp.concatenate([recv_at, here])

    full_ph, gamma_ph = after((full_ph, gamma_ph), (send_index, recv_index))
    scaled = scale_rows(gamma_ph, chi_ph)
    pp_halves = (pp_vertex[:, :128], pp_vertex[:, 128:])
    pieces_1 = gather_rows(*cut(full_ph, False), between=pp_halves)
    phi_1, outgoing_1 = ph_half(False, send_index, scaled, pieces_1, 4)
    pieces_2 = gather_whole(after(cut(full_ph, True)[0], pieces_1), outgoing_1)
    came_1 = exchange(outgoing_1)
    phi_2, outgoing_2 = ph_half(True, send_index, scaled, pieces_2, NEAR)
    pp_pieces = gather_rows(*after(pp_halves, pieces_2), between=outgoing_2)
    came_2 = exchange(outgoing_2)
    held = tuple(hold(x, FAR) for x in pp_pieces[2:6])
    leaving = pp_whole(
        recv_index, came_1, came_2, chi_pp, pp_pieces[:2] + held + pp_pieces[6:]
    )
    base = base_sum(gamma_ph, phi_1, phi_2)
    return last_sum(send_index, base, exchange(leaving))


def solution(mesh):
    placed = (
        P("boson", "block", None),
        P("boson", "block", None),
        P("boson", None),
        P("boson", "block", None),
        P("boson", None),
        P(),
    )
    return jax.shard_map(
        local, mesh=mesh, in_specs=placed, out_specs=P("boson", "block", None), check_vma=False
    )
```

```python
import jax
import jax.numpy as jnp
from jax import lax
from jax.experimental import pallas as pl
from jax.experimental.pallas import tpu as pltpu
from jax.sharding import PartitionSpec as P

CB = 8
RS = 4
CAP = 3
ITEMS = RS * CB
MIB = 1 << 20
NEAR, LATE = 20, 20
BF16 = jnp.bfloat16
F32 = jnp.float32


def low_lanes(rows):
    return lax.broadcasted_iota(jnp.int32, (rows, 128), 1) < 64


def swap_lanes(x):
    return pltpu.roll(x, 64, 1)


def start_all(copies):
    for copy in copies:
        copy.start()
    return copies


def wait_all(copies):
    for copy in copies:
        copy.wait()


def point_loads(sources, targets, sems):
    return [
        start_all(
            [
                pltpu.make_async_copy(x.at[q], y.at[q], sems.at[k, q])
                for k, (x, y) in enumerate(zip(sources, targets))
            ]
        )
        for q in range(4)
    ]


def right_loads(pieces, block_here, right, sems):
    whole = len(pieces) == 5
    where = [(step, 0, half * 256) for step in STEPS for half in range(2)]
    if whole:
        where = [(step, 0, 0) for step in STEPS] + [(STEPS[3], 128, 0)]
    loads = []
    for q in range(4):
        copies = []
        for k, (piece, (step, offset, column)) in enumerate(zip(pieces, where)):
            rows, width = piece.shape[1:]
            start = pl.multiple_of(lax.rem(block_here + step, 4) * 256 + offset, 128)
            to = right.at[q, pl.ds(start, rows), column : column + width]
            copies.append(pltpu.make_async_copy(piece.at[q], to, sems.at[k, q]))
        loads.append(start_all(copies))
    return loads


def pack(second, index, q, half, part, slots):
    low = low_lanes(32)
    for r in range(RS):
        for m in range(2):
            pair = part[r * 64 : r * 64 + 64, m * 128 : m * 128 + 128]
            top, bottom = pair[:32], swap_lanes(pair[32:])
            item = q * ITEMS + r * CB + half * 4 + m * 2
            ahead, behind = (1, 0) if second else (0, 1)
            slots[index[item + ahead]] = jnp.where(low, top, bottom).astype(BF16)
            slots[index[item + behind]] = jnp.where(low, bottom, top).astype(BF16)


def tile_rows(r, c):
    straight, crossed = r * 64 + c % 2 * 32, r * 64 + 32 - c % 2 * 32
    return slice(straight, straight + 32), slice(crossed, crossed + 32)


def cut_kernel(high_lanes, x, *refs):
    n = (len(refs) - 3) // 2
    outs, x_here, outs_here, in_sems, out_sems = refs[:n], refs[n], refs[n + 1 : -2], refs[-2], refs[-1]
    loads = point_loads([x], [x_here], in_sems)
    low = low_lanes(256)
    stores = []
    for q in range(4):
        wait_all(loads[q])
        for m in range(4):
            even = x_here[q, :, m * 256 : m * 256 + 128].astype(F32)
            odd = swap_lanes(x_here[q, :, m * 256 + 128 : m * 256 + 256].astype(F32))
            lanes = jnp.where(low, odd, even) if high_lanes else jnp.where(low, even, odd)
            out = outs_here[m * n // 4]
            to = m * 128 % out.shape[2]
            out[q, :, to : to + 128] = lanes.astype(BF16)
        stores += start_all(
            [
                pltpu.make_async_copy(y.at[q], out.at[q], out_sems.at[k, q])
                for k, (y, out) in enumerate(zip(outs_here, outs))
            ]
        )
    wait_all(stores)


def after(value, others):
    return lax.optimization_barrier((value, others))[0]


def gather_rows(low, high, between=None):
    n = lax.axis_size("block")
    up = [(i, (i + 1) % n) for i in range(n)]
    down = [(i, (i - 1) % n) for i in range(n)]
    below_low = lax.ppermute(low, "block", up)
    above_high = lax.ppermute(high, "block", down)
    below_high = lax.ppermute(high, "block", up)
    above_low = lax.ppermute(low, "block", down)
    near = (below_low, above_high)
    if between is not None:
        near = after(near, between)
    far_low = lax.ppermute(near[0], "block", up)
    far_high = lax.ppermute(near[1], "block", down)
    return low, high, below_low, below_high, above_low, above_high, far_low, far_high


def gather_whole(own, between):
    n = lax.axis_size("block")
    up = [(i, (i + 1) % n) for i in range(n)]
    down = [(i, (i - 1) % n) for i in range(n)]
    half = own.shape[1] // 2
    below = lax.ppermute(own, "block", up)
    above = lax.ppermute(own, "block", down)
    near_low, near_high = after((below[:, :half], above[:, half:]), between)
    return (
        own,
        below,
        above,
        lax.ppermute(near_low, "block", up),
        lax.ppermute(near_high, "block", down),
    )


STEPS = (0, 3, 1, 2)


def product(lhs, here, pieces, q, half):
    total = None
    for k, step in enumerate(STEPS):
        start = pl.multiple_of(lax.rem(here + step, 4) * 256, 256)
        block = pieces[2 * k + half][q]
        term = jnp.dot(lhs[:, pl.ds(start, 256)], block, preferred_element_type=F32)
        total = term if total is None else total + term
    return total


def scale_kernel(gamma, chi, out):
    row = chi[pl.ds(pl.program_id(0), 1), :]
    out[0] = (gamma[0].astype(F32) * row).astype(BF16)


def ph_kernel(second, index, scaled, *refs):
    n = 5 if second else 8
    pieces, (phi_out, slots_out, phi, slots, out_sems) = refs[:n], refs[n : n + 5]
    if second:
        left, right, left_sems, in_sems = refs[n + 5 :]
        left_loads = point_loads([scaled], [left], left_sems)
        loads = right_loads(pieces, index[128], right, in_sems)
    stores = []
    for q in range(4):
        if second:
            wait_all(left_loads[q] + loads[q])
        for half in range(2):
            columns = slice(half * 256, half * 256 + 256)
            if second:
                part = jnp.dot(left[q], right[q, :, columns], preferred_element_type=F32)
            else:
                part = product(scaled.at[q], index[128], pieces, q, half)
            phi[q, :, columns] = part
            pack(second, index, q, half, part, slots)
        stores += start_all([pltpu.make_async_copy(phi.at[q], phi_out.at[q], out_sems.at[q])])
    stores += start_all([pltpu.make_async_copy(slots, slots_out, out_sems.at[4])])
    wait_all(stores)


def pp_kernel(second, index, first_in, second_in, chi, *refs):
    n = 5 if second else 8
    pieces, slots_out = refs[:n], refs[n]
    right, first, last, slots, lhs, in_sems, slot_sems = refs[n + 1 :]
    arrivals = start_all(
        [
            pltpu.make_async_copy(first_in, first, slot_sems.at[0]),
            pltpu.make_async_copy(second_in, last, slot_sems.at[1]),
        ]
    )
    loads = right_loads(pieces, index[128], right, in_sems)
    wait_all(arrivals)
    low = low_lanes(32)
    for p in range(4):
        row = chi[p : p + 1, :]
        for r in range(RS):
            for c in range(CB):
                slot = index[p * ITEMS + r * CB + c]
                a, b = first[slot].astype(F32), last[slot].astype(F32)
                columns = slice(c * 128, c * 128 + 128)
                straight, crossed = tile_rows(r, c)
                scale = row[:, columns]
                lhs[straight, columns] = (jnp.where(low, a, b) * scale).astype(BF16)
                lhs[crossed, columns] = (swap_lanes(jnp.where(low, b, a)) * scale).astype(BF16)
        wait_all(loads[p])
        for half in range(2):
            columns = slice(half * 256, half * 256 + 256)
            part = jnp.dot(lhs[...], right[p, :, columns], preferred_element_type=F32)
            pack(second, index, p, half, part, slots)
    wait_all(start_all([pltpu.make_async_copy(slots, slots_out, slot_sems.at[2])]))


def base_kernel(index, gamma, first, second, came, out):
    q = pl.program_id(0)
    low = low_lanes(256)
    for m in range(4):
        a = first[0, :, m * 128 : m * 128 + 128]
        b = second[0, :, m * 128 : m * 128 + 128]
        for c, phi in ((2 * m, jnp.where(low, a, b)), (2 * m + 1, swap_lanes(jnp.where(low, b, a)))):
            columns = slice(c * 128, c * 128 + 128)
            base = gamma[0, :, columns].astype(F32) + phi
            for r in range(RS):
                back = came[index[q * ITEMS + r * CB + c]].astype(F32)
                straight, crossed = tile_rows(r, c)
                out[0, straight, columns] = base[straight] + jnp.where(low[:32], back, 0.0)
                out[0, crossed, columns] = base[crossed] + swap_lanes(jnp.where(low[:32], 0.0, back))


def sum_kernel(index, base_in, came, out, base, total, in_sems, out_sems):
    loads = point_loads([base_in], [base], in_sems)
    low = low_lanes(32)
    stores = []
    for q in range(4):
        wait_all(loads[q])
        for r in range(RS):
            for c in range(CB):
                columns = slice(c * 128, c * 128 + 128)
                straight, crossed = tile_rows(r, c)
                back = came[index[q * ITEMS + r * CB + c]].astype(F32)
                for rows, term in (
                    (straight, jnp.where(low, 0.0, back)),
                    (crossed, swap_lanes(jnp.where(low, back, 0.0))),
                ):
                    total[q, rows, columns] = (base[q, rows, columns] + term).astype(BF16)
        stores += start_all([pltpu.make_async_copy(total.at[q], out.at[q], out_sems.at[q])])
    wait_all(stores)


def point_spec(rows, columns):
    return pl.BlockSpec((1, rows, columns), lambda q, *index: (q, 0, 0))


def whole_spec(shape):
    return pl.BlockSpec(shape, lambda q, *index: (0,) * len(shape))


def call(
    kernel, index, operands, in_specs, out_specs, out_shape, scratch, us, grant, free=(), **other
):
    return pl.pallas_call(
        kernel,
        grid_spec=pltpu.PrefetchScalarGridSpec(
            num_scalar_prefetch=len(index),
            grid=other.get("grid", (4,)),
            in_specs=in_specs,
            out_specs=out_specs,
            scratch_shapes=scratch,
        ),
        out_shape=out_shape,
        compiler_params=pltpu.CompilerParams(vmem_limit_bytes=grant * MIB),
        cost_estimate=pl.CostEstimate(
            flops=int(us * 1e9), bytes_accessed=int(us * 3e6), transcendentals=0
        ),
    )(
        *index,
        *(
            x if k in free else pltpu.with_memory_space_constraint(x, pltpu.HBM)
            for k, x in enumerate(operands)
        ),
    )


def plan(relabel, points, boson_here, block_here):
    nboson = lax.axis_size("boson")
    item_total = points * ITEMS
    own_targets = lax.dynamic_slice(
        relabel, (boson_here * points, block_here * RS, 0), (points, RS, CB)
    ).reshape(item_total)
    shifts = (own_targets // points - boson_here) % nboson
    item_range = jnp.arange(item_total, dtype=jnp.int32)
    target = own_targets % points * ITEMS + item_range % ITEMS
    earlier = (shifts[None, :] == shifts[:, None]) & (item_range[None, :] < item_range[:, None])
    rank = jnp.sum(earlier.astype(jnp.int32), axis=1)
    send = (boson_here + shifts) % nboson * CAP + rank
    recv = (boson_here - shifts) % nboson * CAP + rank
    recv_at = jnp.sum(
        (target[None, :] == item_range[:, None]).astype(jnp.int32) * recv[None, :], axis=1
    )
    return send, recv_at


def exchange(slots):
    nboson = lax.axis_size("boson")
    tile = slots.shape[1:]
    return lax.all_to_all(
        slots.reshape((nboson, CAP) + tile), "boson", split_axis=0, concat_axis=0, tiled=True
    ).reshape(slots.shape)


HALF_TILES = (64 * CAP, 32, 128)
ROWS = point_spec(256, 1024)
CHI = whole_spec((4, 1024))


def specs(pieces):
    return [point_spec(*x.shape[1:]) for x in pieces]


ANY = pl.BlockSpec(memory_space=pl.ANY)
NEAR_BY = pl.BlockSpec(memory_space=pltpu.VMEM)
DMA = pltpu.SemaphoreType.DMA


def vmem(x):
    return pltpu.VMEM(x.shape, x.dtype)


def cut(full, high_lanes, pinned=False):
    def kernel(*refs):
        cut_kernel(high_lanes, *refs)

    parts = 1 if high_lanes else 2
    shape = (4, 256, 512 // parts)
    scratch = [vmem(full)] + [pltpu.VMEM(shape, BF16)] * parts + [DMA((1, 4)), DMA((parts, 4))]
    outs = [pltpu.HBM(shape, BF16) if pinned else jax.ShapeDtypeStruct(shape, BF16)] * parts
    return call(kernel, (), (full,), [ANY], [ANY] * parts, outs, scratch, 2, 6, grid=())


def scale_rows(gamma, chi):
    out = jax.ShapeDtypeStruct(gamma.shape, BF16)
    return call(scale_kernel, (), (gamma, chi), [ROWS, CHI], ROWS, out, [], 2, 6)


def ph_half(second, index, scaled, pieces, us):
    def kernel(*refs):
        ph_kernel(second, *refs)

    phi = (4, 256, 512)
    scratch = [pltpu.VMEM(phi, F32), pltpu.VMEM(HALF_TILES, BF16), DMA((5,))]
    if second:
        scratch += [vmem(scaled), pltpu.VMEM((4, 1024, 512), BF16), DMA((1, 4)), DMA((5, 4))]
    return call(
        kernel,
        (index,),
        (scaled,) + pieces,
        [ANY if second else NEAR_BY] * (len(pieces) + 1),
        [ANY] * 2,
        [pltpu.HBM(phi, F32), pltpu.HBM(HALF_TILES, BF16)],
        scratch,
        us,
        14 if second else 8,
        free=() if second else tuple(range(9)),
        grid=(),
    )


def pp_half(second, index, came_1, came_2, chi, pieces, us):
    def kernel(*refs):
        pp_kernel(second, *refs)

    n = len(pieces)
    scratch = [pltpu.VMEM((4, 1024, 512), BF16), vmem(came_1), vmem(came_2)]
    scratch += [pltpu.VMEM(HALF_TILES, BF16), pltpu.VMEM((256, 1024), BF16), DMA((n, 4)), DMA((3,))]
    return call(
        kernel,
        (index,),
        (came_1, came_2, chi) + pieces,
        [ANY, ANY, NEAR_BY] + [ANY] * n,
        ANY,
        pltpu.HBM(HALF_TILES, BF16),
        scratch,
        us,
        16,
        free=(2,) if second else (1, 2),
        grid=(),
    )


def base_sum(index, gamma, phi_1, phi_2, back, us):
    return call(
        base_kernel,
        (index,),
        (gamma, phi_1, phi_2, back),
        [ROWS] + [point_spec(256, 512)] * 2 + [whole_spec(HALF_TILES)],
        ROWS,
        pltpu.HBM(gamma.shape, F32),
        [],
        us,
        16,
        free=(3,),
    )


def last_sum(index, base, back):
    out = pltpu.HBM(base.shape, BF16)
    scratch = [vmem(base), pltpu.VMEM(base.shape, BF16), DMA((1, 4)), DMA((4,))]
    return call(
        sum_kernel,
        (index,),
        (base, back),
        [ANY, NEAR_BY],
        ANY,
        out,
        scratch,
        3,
        10,
        free=(1,),
        grid=(),
    )


def local(gamma_ph, full_ph, chi_ph, pp_vertex, chi_pp, relabel):
    block_here = lax.axis_index("block")
    send, recv_at = plan(relabel, gamma_ph.shape[0], lax.axis_index("boson"), block_here)
    here = jnp.full((8,), block_here, jnp.int32)
    send_index = jnp.concatenate([send, here])
    recv_index = jnp.concatenate([recv_at, here])

    full_ph, gamma_ph = after((full_ph, gamma_ph), (send_index, recv_index))
    scaled = scale_rows(gamma_ph, chi_ph)
    pp_first, pp_second = cut(pp_vertex, False, True), cut(pp_vertex, True, True)[0]
    pieces_1 = gather_rows(*cut(full_ph, False), between=(pp_first, pp_second))
    phi_1, outgoing_1 = ph_half(False, send_index, scaled, pieces_1, 4)
    pieces_2 = gather_whole(after(cut(full_ph, True)[0], pieces_1), outgoing_1)
    came_1 = exchange(outgoing_1)
    phi_2, outgoing_2 = ph_half(True, send_index, scaled, pieces_2, NEAR)
    pieces_3 = gather_rows(*after(pp_first, pieces_2), between=outgoing_2)
    came_2 = exchange(outgoing_2)
    leaving_1 = pp_half(False, recv_index, came_1, came_2, chi_pp, pieces_3, 5)
    pieces_4 = gather_whole(after(pp_second, pieces_3), leaving_1)
    back_1 = exchange(leaving_1)
    leaving_2 = pp_half(True, recv_index, came_1, came_2, chi_pp, pieces_4, LATE)
    base = base_sum(send_index, gamma_ph, phi_1, phi_2, back_1, 5)
    return last_sum(send_index, base, exchange(leaving_2))


def solution(mesh):
    placed = (
        P("boson", "block", None),
        P("boson", "block", None),
        P("boson", None),
        P("boson", "block", None),
        P("boson", None),
        P(),
    )
    return jax.shard_map(
        local, mesh=mesh, in_specs=placed, out_specs=P("boson", "block", None), check_vma=False
    )
```

```python
import jax
import jax.numpy as jnp
from jax import lax
from jax.experimental import pallas as pl
from jax.experimental.pallas import tpu as pltpu
from jax.sharding import PartitionSpec as P

CB = 8
RS = 4
CAP = 3
ITEMS = RS * CB
MIB = 1 << 20
NEAR, FAR = 20, 14
BF16 = jnp.bfloat16
F32 = jnp.float32


def low_lanes(rows):
    return lax.broadcasted_iota(jnp.int32, (rows, 128), 1) < 64


def swap_lanes(x):
    return pltpu.roll(x, 64, 1)


def start_all(copies):
    for copy in copies:
        copy.start()
    return copies


def wait_all(copies):
    for copy in copies:
        copy.wait()


def point_loads(sources, targets, sems):
    return [
        start_all(
            [
                pltpu.make_async_copy(x.at[q], y.at[q], sems.at[k, q])
                for k, (x, y) in enumerate(zip(sources, targets))
            ]
        )
        for q in range(4)
    ]


def right_loads(pieces, block_here, right, sems):
    where = [(step, offset) for step in STEPS for offset in (0, 128)]
    where = [(s, o) for k, (s, o) in enumerate(where) if len(pieces) == 8 or o == 0 or k == 7]
    loads = []
    for q in range(4):
        copies = []
        for k, (piece, (step, offset)) in enumerate(zip(pieces, where)):
            start = pl.multiple_of(lax.rem(block_here + step, 4) * 256 + offset, 128)
            to = right.at[q, pl.ds(start, piece.shape[1])]
            copies.append(pltpu.make_async_copy(piece.at[q], to, sems.at[k, q]))
        loads.append(start_all(copies))
    return loads


def cut_kernel(high_lanes, x, *refs):
    n = (len(refs) - 3) // 2
    outs, x_here, outs_here, in_sems, out_sems = refs[:n], refs[n], refs[n + 1 : -2], refs[-2], refs[-1]
    loads = point_loads([x], [x_here], in_sems)
    low = low_lanes(256)
    stores = []
    for q in range(4):
        wait_all(loads[q])
        for m in range(4):
            even = x_here[q, :, m * 256 : m * 256 + 128].astype(F32)
            odd = swap_lanes(x_here[q, :, m * 256 + 128 : m * 256 + 256].astype(F32))
            lanes = jnp.where(low, odd, even) if high_lanes else jnp.where(low, even, odd)
            out = outs_here[m * n // 4]
            to = m * 128 % out.shape[2]
            out[q, :, to : to + 128] = lanes.astype(BF16)
        stores += start_all(
            [
                pltpu.make_async_copy(y.at[q], out.at[q], out_sems.at[k, q])
                for k, (y, out) in enumerate(zip(outs_here, outs))
            ]
        )
    wait_all(stores)


def hold_kernel(x, out):
    pass


def after(value, others):
    return lax.optimization_barrier((value, others))[0]


def gather_rows(low, high, between=None):
    n = lax.axis_size("block")
    up = [(i, (i + 1) % n) for i in range(n)]
    down = [(i, (i - 1) % n) for i in range(n)]
    below_low = lax.ppermute(low, "block", up)
    above_high = lax.ppermute(high, "block", down)
    below_high = lax.ppermute(high, "block", up)
    above_low = lax.ppermute(low, "block", down)
    near = (below_low, above_high)
    if between is not None:
        near = after(near, between)
    far_low = lax.ppermute(near[0], "block", up)
    far_high = lax.ppermute(near[1], "block", down)
    return low, high, below_low, below_high, above_low, above_high, far_low, far_high


def gather_whole(own, between):
    n = lax.axis_size("block")
    up = [(i, (i + 1) % n) for i in range(n)]
    down = [(i, (i - 1) % n) for i in range(n)]
    half = own.shape[1] // 2
    below = lax.ppermute(own, "block", up)
    above = lax.ppermute(own, "block", down)
    near_low, near_high = after((below[:, :half], above[:, half:]), between)
    return (
        own,
        below,
        above,
        lax.ppermute(near_low, "block", up),
        lax.ppermute(near_high, "block", down),
    )


STEPS = (0, 3, 1, 2)


def product(lhs, here, pieces, q, half):
    total = None
    for k, step in enumerate(STEPS):
        start = pl.multiple_of(lax.rem(here + step, 4) * 256, 256)
        block = pieces[2 * k + half][q]
        term = jnp.dot(lhs[:, pl.ds(start, 256)], block, preferred_element_type=F32)
        total = term if total is None else total + term
    return total


def scale_kernel(gamma, chi, out):
    row = chi[pl.ds(pl.program_id(0), 1), :]
    out[0] = (gamma[0].astype(F32) * row).astype(BF16)


def ph_kernel(second, index, scaled, *refs):
    n = 5 if second else 8
    pieces, (phi_out, slots_out, phi, slots, out_sems) = refs[:n], refs[n : n + 5]
    if second:
        left, right, left_sems, in_sems = refs[n + 5 :]
        left_loads = point_loads([scaled], [left], left_sems)
        loads = right_loads(pieces, index[128], right, in_sems)
    low = low_lanes(32)
    stores = []
    for q in range(4):
        if second:
            wait_all(left_loads[q] + loads[q])
        for half in range(2):
            columns = slice(half * 256, half * 256 + 256)
            if second:
                part = jnp.dot(left[q], right[q, :, columns], preferred_element_type=F32)
            else:
                part = product(scaled.at[q], index[128], pieces, q, half)
            phi[q, :, columns] = part
            for r in range(RS):
                for m in range(2):
                    pair = part[r * 64 : r * 64 + 64, m * 128 : m * 128 + 128]
                    top, bottom = pair[:32], swap_lanes(pair[32:])
                    item = q * ITEMS + r * CB + half * 4 + m * 2
                    ahead, behind = (1, 0) if second else (0, 1)
                    slots[index[item + ahead]] = jnp.where(low, top, bottom).astype(BF16)
                    slots[index[item + behind]] = jnp.where(low, bottom, top).astype(BF16)
        stores += start_all([pltpu.make_async_copy(phi.at[q], phi_out.at[q], out_sems.at[q])])
    stores += start_all([pltpu.make_async_copy(slots, slots_out, out_sems.at[4])])
    wait_all(stores)


def pp_kernel(index, first_in, second, chi, *refs):
    pieces, slots_out = refs[:8], refs[8]
    right, first, slots, lhs, in_sems, slot_sems = refs[9:]
    arrivals = start_all([pltpu.make_async_copy(first_in, first, slot_sems.at[0])])
    loads = right_loads(pieces, index[128], right, in_sems)
    wait_all(arrivals)
    low = low_lanes(32)
    for p in range(4):
        row = chi[p : p + 1, :]
        for r in range(RS):
            for c in range(CB):
                slot = index[p * ITEMS + r * CB + c]
                a, b = first[slot].astype(F32), second[slot].astype(F32)
                scale = row[:, c * 128 : c * 128 + 128]
                straight = (jnp.where(low, a, b) * scale).astype(BF16)
                crossed = (swap_lanes(jnp.where(low, b, a)) * scale).astype(BF16)
                top = r * 64 + c % 2 * 32
                other = r * 64 + 32 - c % 2 * 32
                lhs[top : top + 32, c * 128 : c * 128 + 128] = straight
                lhs[other : other + 32, c * 128 : c * 128 + 128] = crossed
        wait_all(loads[p])
        for half in range(2):
            columns = slice(half * 512, half * 512 + 512)
            phi = jnp.dot(lhs[...], right[p, :, columns], preferred_element_type=F32).astype(BF16)
            for r in range(RS):
                for c in range(4):
                    slot = index[p * ITEMS + r * CB + half * 4 + c]
                    slots[slot] = phi[r * 64 : r * 64 + 64, c * 128 : c * 128 + 128]
    wait_all(start_all([pltpu.make_async_copy(slots, slots_out, slot_sems.at[1])]))


def base_kernel(gamma, first, second, out):
    low = low_lanes(256)
    for m in range(4):
        a = first[0, :, m * 128 : m * 128 + 128]
        b = second[0, :, m * 128 : m * 128 + 128]
        for c, phi in ((2 * m, jnp.where(low, a, b)), (2 * m + 1, swap_lanes(jnp.where(low, b, a)))):
            columns = slice(c * 128, c * 128 + 128)
            out[0, :, columns] = gamma[0, :, columns].astype(F32) + phi


def sum_kernel(index, base_in, came, out, base, total, in_sems, out_sems):
    loads = point_loads([base_in], [base], in_sems)
    stores = []
    for q in range(4):
        wait_all(loads[q])
        for r in range(RS):
            for c in range(CB):
                rows, columns = slice(r * 64, r * 64 + 64), slice(c * 128, c * 128 + 128)
                back = came[index[q * ITEMS + r * CB + c]].astype(F32)
                total[q, rows, columns] = (base[q, rows, columns] + back).astype(BF16)
        stores += start_all([pltpu.make_async_copy(total.at[q], out.at[q], out_sems.at[q])])
    wait_all(stores)


def point_spec(rows, columns):
    return pl.BlockSpec((1, rows, columns), lambda q, *index: (q, 0, 0))


def whole_spec(shape):
    return pl.BlockSpec(shape, lambda q, *index: (0,) * len(shape))


def call(
    kernel, index, operands, in_specs, out_specs, out_shape, scratch, us, grant, free=(), **other
):
    return pl.pallas_call(
        kernel,
        grid_spec=pltpu.PrefetchScalarGridSpec(
            num_scalar_prefetch=len(index),
            grid=other.get("grid", (4,)),
            in_specs=in_specs,
            out_specs=out_specs,
            scratch_shapes=scratch,
        ),
        out_shape=out_shape,
        compiler_params=pltpu.CompilerParams(vmem_limit_bytes=grant * MIB),
        cost_estimate=pl.CostEstimate(
            flops=int(us * 1e9), bytes_accessed=int(us * 3e6), transcendentals=0
        ),
        input_output_aliases=other.get("aliases", {}),
    )(
        *index,
        *(
            x if k in free else pltpu.with_memory_space_constraint(x, pltpu.HBM)
            for k, x in enumerate(operands)
        ),
    )


def plan(relabel, points, boson_here, block_here):
    nboson = lax.axis_size("boson")
    item_total = points * ITEMS
    own_targets = lax.dynamic_slice(
        relabel, (boson_here * points, block_here * RS, 0), (points, RS, CB)
    ).reshape(item_total)
    shifts = (own_targets // points - boson_here) % nboson
    item_range = jnp.arange(item_total, dtype=jnp.int32)
    target = own_targets % points * ITEMS + item_range % ITEMS
    earlier = (shifts[None, :] == shifts[:, None]) & (item_range[None, :] < item_range[:, None])
    rank = jnp.sum(earlier.astype(jnp.int32), axis=1)
    send = (boson_here + shifts) % nboson * CAP + rank
    recv = (boson_here - shifts) % nboson * CAP + rank
    recv_at = jnp.sum(
        (target[None, :] == item_range[:, None]).astype(jnp.int32) * recv[None, :], axis=1
    )
    return send, recv_at


def exchange(slots):
    nboson = lax.axis_size("boson")
    tile = slots.shape[1:]
    return lax.all_to_all(
        slots.reshape((nboson, CAP) + tile), "boson", split_axis=0, concat_axis=0, tiled=True
    ).reshape(slots.shape)


HALF_TILES = (64 * CAP, 32, 128)
TILES = (64 * CAP, 64, 128)
ROWS = point_spec(256, 1024)
CHI = whole_spec((4, 1024))


def specs(pieces):
    return [point_spec(*x.shape[1:]) for x in pieces]


ANY = pl.BlockSpec(memory_space=pl.ANY)
NEAR_BY = pl.BlockSpec(memory_space=pltpu.VMEM)
DMA = pltpu.SemaphoreType.DMA


def vmem(x):
    return pltpu.VMEM(x.shape, x.dtype)


def cut(full, high_lanes):
    def kernel(*refs):
        cut_kernel(high_lanes, *refs)

    parts = 1 if high_lanes else 2
    shape = (4, 256, 512 // parts)
    scratch = [vmem(full)] + [pltpu.VMEM(shape, BF16)] * parts + [DMA((1, 4)), DMA((parts, 4))]
    outs = [jax.ShapeDtypeStruct(shape, BF16)] * parts
    return call(kernel, (), (full,), [ANY], [ANY] * parts, outs, scratch, 2, 6, grid=())


def scale_rows(gamma, chi):
    out = jax.ShapeDtypeStruct(gamma.shape, BF16)
    return call(scale_kernel, (), (gamma, chi), [ROWS, CHI], ROWS, out, [], 2, 6)


def hold(x, us):
    anywhere = pl.BlockSpec(memory_space=pl.ANY)
    out = pltpu.HBM(x.shape, x.dtype)
    return call(
        hold_kernel, (), (x,), [anywhere], anywhere, out, [], us, 1, grid=(1,), aliases={0: 0}
    )


def ph_half(second, index, scaled, pieces, us):
    def kernel(*refs):
        ph_kernel(second, *refs)

    phi = (4, 256, 512)
    scratch = [pltpu.VMEM(phi, F32), pltpu.VMEM(HALF_TILES, BF16), DMA((5,))]
    if second:
        scratch += [vmem(scaled), pltpu.VMEM((4, 1024, 512), BF16), DMA((1, 4)), DMA((5, 4))]
    return call(
        kernel,
        (index,),
        (scaled,) + pieces,
        [ANY if second else NEAR_BY] * (len(pieces) + 1),
        [ANY] * 2,
        [pltpu.HBM(phi, F32), pltpu.HBM(HALF_TILES, BF16)],
        scratch,
        us,
        14 if second else 8,
        free=() if second else tuple(range(9)),
        grid=(),
    )


def pp_whole(index, came_1, came_2, chi, pieces):
    scratch = [pltpu.VMEM((4, 1024, 1024), BF16), vmem(came_1), pltpu.VMEM(TILES, BF16)]
    scratch += [pltpu.VMEM((256, 1024), BF16), DMA((8, 4)), DMA((2,))]
    return call(
        pp_kernel,
        (index,),
        (came_1, came_2, chi) + pieces,
        [ANY, NEAR_BY, NEAR_BY] + [ANY] * 8,
        ANY,
        pltpu.HBM(TILES, BF16),
        scratch,
        5,
        20,
        free=(1, 2),
        grid=(),
    )


def base_sum(gamma, phi_1, phi_2):
    return call(
        base_kernel,
        (),
        (gamma, phi_1, phi_2),
        [ROWS] + [point_spec(256, 512)] * 2,
        ROWS,
        pltpu.HBM(gamma.shape, F32),
        [],
        4,
        10,
    )


def last_sum(index, base, back):
    out = pltpu.HBM(base.shape, BF16)
    scratch = [vmem(base), pltpu.VMEM(base.shape, BF16), DMA((1, 4)), DMA((4,))]
    return call(
        sum_kernel,
        (index,),
        (base, back),
        [ANY, NEAR_BY],
        ANY,
        out,
        scratch,
        3,
        10,
        free=(1,),
        grid=(),
    )


def local(gamma_ph, full_ph, chi_ph, pp_vertex, chi_pp, relabel):
    block_here = lax.axis_index("block")
    send, recv_at = plan(relabel, gamma_ph.shape[0], lax.axis_index("boson"), block_here)
    here = jnp.full((8,), block_here, jnp.int32)
    send_index = jnp.concatenate([send, here])
    recv_index = jnp.concatenate([recv_at, here])

    full_ph, gamma_ph = after((full_ph, gamma_ph), (send_index, recv_index))
    scaled = scale_rows(gamma_ph, chi_ph)
    pp_halves = (pp_vertex[:, :128], pp_vertex[:, 128:])
    pieces_1 = gather_rows(*cut(full_ph, False), between=pp_halves)
    phi_1, outgoing_1 = ph_half(False, send_index, scaled, pieces_1, 4)
    pieces_2 = gather_whole(after(cut(full_ph, True)[0], pieces_1), outgoing_1)
    came_1 = exchange(outgoing_1)
    phi_2, outgoing_2 = ph_half(True, send_index, scaled, pieces_2, NEAR)
    pp_pieces = gather_rows(*after(pp_halves, pieces_2), between=outgoing_2)
    came_2 = exchange(outgoing_2)
    held = tuple(hold(x, FAR) if k in (1, 2) else x for k, x in enumerate(pp_pieces[2:6]))
    leaving = pp_whole(
        recv_index, came_1, came_2, chi_pp, pp_pieces[:2] + held + pp_pieces[6:]
    )
    base = base_sum(gamma_ph, phi_1, phi_2)
    return last_sum(send_index, base, exchange(leaving))


def solution(mesh):
    placed = (
        P("boson", "block", None),
        P("boson", "block", None),
        P("boson", None),
        P("boson", "block", None),
        P("boson", None),
        P(),
    )
    return jax.shard_map(
        local, mesh=mesh, in_specs=placed, out_specs=P("boson", "block", None), check_vma=False
    )
```

```python
import jax
import jax.numpy as jnp
from jax import lax
from jax.experimental import pallas as pl
from jax.experimental.pallas import tpu as pltpu
from jax.sharding import PartitionSpec as P

CB = 8
RS = 4
CAP = 3
ITEMS = RS * CB
MIB = 1 << 20
NEAR, FAR = 20, 14
BF16 = jnp.bfloat16
F32 = jnp.float32


def low_lanes(rows):
    return lax.broadcasted_iota(jnp.int32, (rows, 128), 1) < 64


def swap_lanes(x):
    return pltpu.roll(x, 64, 1)


def start_all(copies):
    for copy in copies:
        copy.start()
    return copies


def wait_all(copies):
    for copy in copies:
        copy.wait()


def point_loads(sources, targets, sems):
    return [
        start_all(
            [
                pltpu.make_async_copy(x.at[q], y.at[q], sems.at[k, q])
                for k, (x, y) in enumerate(zip(sources, targets))
            ]
        )
        for q in range(4)
    ]


def right_loads(pieces, block_here, right, sems):
    where = [(step, offset) for step in STEPS for offset in (0, 128)]
    where = [(s, o) for k, (s, o) in enumerate(where) if len(pieces) == 8 or o == 0 or k == 7]
    loads = []
    for q in range(4):
        copies = []
        for k, (piece, (step, offset)) in enumerate(zip(pieces, where)):
            start = pl.multiple_of(lax.rem(block_here + step, 4) * 256 + offset, 128)
            to = right.at[q, pl.ds(start, piece.shape[1])]
            copies.append(pltpu.make_async_copy(piece.at[q], to, sems.at[k, q]))
        loads.append(start_all(copies))
    return loads


def cut_kernel(high_lanes, x, *refs):
    n = (len(refs) - 3) // 2
    outs, x_here, outs_here, in_sems, out_sems = refs[:n], refs[n], refs[n + 1 : -2], refs[-2], refs[-1]
    loads = point_loads([x], [x_here], in_sems)
    low = low_lanes(256)
    stores = []
    for q in range(4):
        wait_all(loads[q])
        for m in range(4):
            even = x_here[q, :, m * 256 : m * 256 + 128].astype(F32)
            odd = swap_lanes(x_here[q, :, m * 256 + 128 : m * 256 + 256].astype(F32))
            lanes = jnp.where(low, odd, even) if high_lanes else jnp.where(low, even, odd)
            out = outs_here[m * n // 4]
            to = m * 128 % out.shape[2]
            out[q, :, to : to + 128] = lanes.astype(BF16)
        stores += start_all(
            [
                pltpu.make_async_copy(y.at[q], out.at[q], out_sems.at[k, q])
                for k, (y, out) in enumerate(zip(outs_here, outs))
            ]
        )
    wait_all(stores)


def hold_kernel(x, out):
    pass


def after(value, others):
    return lax.optimization_barrier((value, others))[0]


def gather_rows(low, high, between=None):
    n = lax.axis_size("block")
    up = [(i, (i + 1) % n) for i in range(n)]
    down = [(i, (i - 1) % n) for i in range(n)]
    below_low = lax.ppermute(low, "block", up)
    above_high = lax.ppermute(high, "block", down)
    below_high = lax.ppermute(high, "block", up)
    above_low = lax.ppermute(low, "block", down)
    near = (below_low, above_high)
    if between is not None:
        near = after(near, between)
    far_low = lax.ppermute(near[0], "block", up)
    far_high = lax.ppermute(near[1], "block", down)
    return low, high, below_low, below_high, above_low, above_high, far_low, far_high


def gather_whole(own, between):
    n = lax.axis_size("block")
    up = [(i, (i + 1) % n) for i in range(n)]
    down = [(i, (i - 1) % n) for i in range(n)]
    half = own.shape[1] // 2
    below = lax.ppermute(own, "block", up)
    above = lax.ppermute(own, "block", down)
    near_low, near_high = after((below[:, :half], above[:, half:]), between)
    return (
        own,
        below,
        above,
        lax.ppermute(near_low, "block", up),
        lax.ppermute(near_high, "block", down),
    )


STEPS = (0, 3, 1, 2)


def product(lhs, here, pieces, q, half):
    total = None
    for k, step in enumerate(STEPS):
        start = pl.multiple_of(lax.rem(here + step, 4) * 256, 256)
        block = pieces[2 * k + half][q]
        term = jnp.dot(lhs[:, pl.ds(start, 256)], block, preferred_element_type=F32)
        total = term if total is None else total + term
    return total


def scale_kernel(gamma, chi, out):
    row = chi[pl.ds(pl.program_id(0), 1), :]
    out[0] = (gamma[0].astype(F32) * row).astype(BF16)


def ph_kernel(second, index, scaled, *refs):
    n = 5 if second else 8
    pieces, (phi_out, slots_out, phi, slots, out_sems) = refs[:n], refs[n : n + 5]
    if second:
        left, right, left_sems, in_sems = refs[n + 5 :]
        left_loads = point_loads([scaled], [left], left_sems)
        loads = right_loads(pieces, index[128], right, in_sems)
    low = low_lanes(32)
    stores = []
    for q in range(4):
        if second:
            wait_all(left_loads[q] + loads[q])
        for half in range(2):
            columns = slice(half * 256, half * 256 + 256)
            if second:
                part = jnp.dot(left[q], right[q, :, columns], preferred_element_type=F32)
            else:
                part = product(scaled.at[q], index[128], pieces, q, half)
            phi[q, :, columns] = part
            for r in range(RS):
                for m in range(2):
                    pair = part[r * 64 : r * 64 + 64, m * 128 : m * 128 + 128]
                    top, bottom = pair[:32], swap_lanes(pair[32:])
                    item = q * ITEMS + r * CB + half * 4 + m * 2
                    ahead, behind = (1, 0) if second else (0, 1)
                    slots[index[item + ahead]] = jnp.where(low, top, bottom).astype(BF16)
                    slots[index[item + behind]] = jnp.where(low, bottom, top).astype(BF16)
        stores += start_all([pltpu.make_async_copy(phi.at[q], phi_out.at[q], out_sems.at[q])])
    stores += start_all([pltpu.make_async_copy(slots, slots_out, out_sems.at[4])])
    wait_all(stores)


def pp_kernel(index, first_in, second, chi, *refs):
    pieces, slots_out = refs[:8], refs[8]
    right, first, tiles, lhs, in_sems, slot_sems = refs[9:]
    arrivals = start_all([pltpu.make_async_copy(first_in, first, slot_sems.at[0])])
    loads = right_loads(pieces, index[128], right, in_sems)
    wait_all(arrivals)
    low = low_lanes(32)
    for p in range(4):
        row = chi[p : p + 1, :]
        for r in range(RS):
            for c in range(CB):
                slot = index[p * ITEMS + r * CB + c]
                a, b = first[slot].astype(F32), second[slot].astype(F32)
                scale = row[:, c * 128 : c * 128 + 128]
                straight = (jnp.where(low, a, b) * scale).astype(BF16)
                crossed = (swap_lanes(jnp.where(low, b, a)) * scale).astype(BF16)
                top = r * 64 + c % 2 * 32
                other = r * 64 + 32 - c % 2 * 32
                lhs[top : top + 32, c * 128 : c * 128 + 128] = straight
                lhs[other : other + 32, c * 128 : c * 128 + 128] = crossed
        wait_all(loads[p])
        for half in range(2):
            columns = slice(half * 512, half * 512 + 512)
            phi = jnp.dot(lhs[...], right[p, :, columns], preferred_element_type=F32).astype(BF16)
            for r in range(RS):
                for c in range(4):
                    item = p * ITEMS + r * CB + half * 4 + c
                    tiles[item] = phi[r * 64 : r * 64 + 64, c * 128 : c * 128 + 128]
                    to = slots_out.at[index[item]]
                    pltpu.make_async_copy(tiles.at[item], to, slot_sems.at[1]).start()
    pltpu.make_async_copy(tiles, slots_out.at[: 4 * ITEMS], slot_sems.at[1]).wait()


def base_kernel(gamma, first, second, out):
    low = low_lanes(256)
    for m in range(4):
        a = first[0, :, m * 128 : m * 128 + 128]
        b = second[0, :, m * 128 : m * 128 + 128]
        for c, phi in ((2 * m, jnp.where(low, a, b)), (2 * m + 1, swap_lanes(jnp.where(low, b, a)))):
            columns = slice(c * 128, c * 128 + 128)
            out[0, :, columns] = gamma[0, :, columns].astype(F32) + phi


def sum_kernel(index, base_in, came, out, base, total, in_sems, out_sems):
    loads = point_loads([base_in], [base], in_sems)
    stores = []
    for q in range(4):
        wait_all(loads[q])
        for r in range(RS):
            for c in range(CB):
                rows, columns = slice(r * 64, r * 64 + 64), slice(c * 128, c * 128 + 128)
                back = came[index[q * ITEMS + r * CB + c]].astype(F32)
                total[q, rows, columns] = (base[q, rows, columns] + back).astype(BF16)
        stores += start_all([pltpu.make_async_copy(total.at[q], out.at[q], out_sems.at[q])])
    wait_all(stores)


def point_spec(rows, columns):
    return pl.BlockSpec((1, rows, columns), lambda q, *index: (q, 0, 0))


def whole_spec(shape):
    return pl.BlockSpec(shape, lambda q, *index: (0,) * len(shape))


def call(
    kernel, index, operands, in_specs, out_specs, out_shape, scratch, us, grant, free=(), **other
):
    return pl.pallas_call(
        kernel,
        grid_spec=pltpu.PrefetchScalarGridSpec(
            num_scalar_prefetch=len(index),
            grid=other.get("grid", (4,)),
            in_specs=in_specs,
            out_specs=out_specs,
            scratch_shapes=scratch,
        ),
        out_shape=out_shape,
        compiler_params=pltpu.CompilerParams(vmem_limit_bytes=grant * MIB),
        cost_estimate=pl.CostEstimate(
            flops=int(us * 1e9), bytes_accessed=int(us * 3e6), transcendentals=0
        ),
        input_output_aliases=other.get("aliases", {}),
    )(
        *index,
        *(
            x if k in free else pltpu.with_memory_space_constraint(x, pltpu.HBM)
            for k, x in enumerate(operands)
        ),
    )


def plan(relabel, points, boson_here, block_here):
    nboson = lax.axis_size("boson")
    item_total = points * ITEMS
    own_targets = lax.dynamic_slice(
        relabel, (boson_here * points, block_here * RS, 0), (points, RS, CB)
    ).reshape(item_total)
    shifts = (own_targets // points - boson_here) % nboson
    item_range = jnp.arange(item_total, dtype=jnp.int32)
    target = own_targets % points * ITEMS + item_range % ITEMS
    earlier = (shifts[None, :] == shifts[:, None]) & (item_range[None, :] < item_range[:, None])
    rank = jnp.sum(earlier.astype(jnp.int32), axis=1)
    send = (boson_here + shifts) % nboson * CAP + rank
    recv = (boson_here - shifts) % nboson * CAP + rank
    recv_at = jnp.sum(
        (target[None, :] == item_range[:, None]).astype(jnp.int32) * recv[None, :], axis=1
    )
    return send, recv_at


def exchange(slots):
    nboson = lax.axis_size("boson")
    tile = slots.shape[1:]
    return lax.all_to_all(
        slots.reshape((nboson, CAP) + tile), "boson", split_axis=0, concat_axis=0, tiled=True
    ).reshape(slots.shape)


HALF_TILES = (64 * CAP, 32, 128)
TILES = (64 * CAP, 64, 128)
ROWS = point_spec(256, 1024)
CHI = whole_spec((4, 1024))


def specs(pieces):
    return [point_spec(*x.shape[1:]) for x in pieces]


ANY = pl.BlockSpec(memory_space=pl.ANY)
NEAR_BY = pl.BlockSpec(memory_space=pltpu.VMEM)
DMA = pltpu.SemaphoreType.DMA


def vmem(x):
    return pltpu.VMEM(x.shape, x.dtype)


def cut(full, high_lanes):
    def kernel(*refs):
        cut_kernel(high_lanes, *refs)

    parts = 1 if high_lanes else 2
    shape = (4, 256, 512 // parts)
    scratch = [vmem(full)] + [pltpu.VMEM(shape, BF16)] * parts + [DMA((1, 4)), DMA((parts, 4))]
    outs = [jax.ShapeDtypeStruct(shape, BF16)] * parts
    return call(kernel, (), (full,), [ANY], [ANY] * parts, outs, scratch, 2, 6, grid=())


def scale_rows(gamma, chi):
    out = jax.ShapeDtypeStruct(gamma.shape, BF16)
    return call(scale_kernel, (), (gamma, chi), [ROWS, CHI], ROWS, out, [], 2, 6)


def hold(x, us):
    anywhere = pl.BlockSpec(memory_space=pl.ANY)
    out = pltpu.HBM(x.shape, x.dtype)
    return call(
        hold_kernel, (), (x,), [anywhere], anywhere, out, [], us, 1, grid=(1,), aliases={0: 0}
    )


def ph_half(second, index, scaled, pieces, us):
    def kernel(*refs):
        ph_kernel(second, *refs)

    phi = (4, 256, 512)
    scratch = [pltpu.VMEM(phi, F32), pltpu.VMEM(HALF_TILES, BF16), DMA((5,))]
    if second:
        scratch += [vmem(scaled), pltpu.VMEM((4, 1024, 512), BF16), DMA((1, 4)), DMA((5, 4))]
    return call(
        kernel,
        (index,),
        (scaled,) + pieces,
        [ANY if second else NEAR_BY] * (len(pieces) + 1),
        [ANY] * 2,
        [pltpu.HBM(phi, F32), pltpu.HBM(HALF_TILES, BF16)],
        scratch,
        us,
        14 if second else 8,
        free=() if second else tuple(range(9)),
        grid=(),
    )


def pp_whole(index, came_1, came_2, chi, pieces):
    scratch = [pltpu.VMEM((4, 1024, 1024), BF16), vmem(came_1), pltpu.VMEM((4 * ITEMS, 64, 128), BF16)]
    scratch += [pltpu.VMEM((256, 1024), BF16), DMA((8, 4)), DMA((2,))]
    return call(
        pp_kernel,
        (index,),
        (came_1, came_2, chi) + pieces,
        [ANY, NEAR_BY, NEAR_BY] + [ANY] * 8,
        ANY,
        pltpu.HBM(TILES, BF16),
        scratch,
        5,
        20,
        free=(1, 2),
        grid=(),
    )


def base_sum(gamma, phi_1, phi_2):
    return call(
        base_kernel,
        (),
        (gamma, phi_1, phi_2),
        [ROWS] + [point_spec(256, 512)] * 2,
        ROWS,
        pltpu.HBM(gamma.shape, F32),
        [],
        4,
        10,
    )


def last_sum(index, base, back):
    out = pltpu.HBM(base.shape, BF16)
    scratch = [vmem(base), pltpu.VMEM(base.shape, BF16), DMA((1, 4)), DMA((4,))]
    return call(
        sum_kernel,
        (index,),
        (base, back),
        [ANY, NEAR_BY],
        ANY,
        out,
        scratch,
        3,
        10,
        free=(1,),
        grid=(),
    )


def local(gamma_ph, full_ph, chi_ph, pp_vertex, chi_pp, relabel):
    block_here = lax.axis_index("block")
    send, recv_at = plan(relabel, gamma_ph.shape[0], lax.axis_index("boson"), block_here)
    here = jnp.full((8,), block_here, jnp.int32)
    send_index = jnp.concatenate([send, here])
    recv_index = jnp.concatenate([recv_at, here])

    full_ph, gamma_ph = after((full_ph, gamma_ph), (send_index, recv_index))
    scaled = scale_rows(gamma_ph, chi_ph)
    pp_halves = (pp_vertex[:, :128], pp_vertex[:, 128:])
    pieces_1 = gather_rows(*cut(full_ph, False), between=pp_halves)
    phi_1, outgoing_1 = ph_half(False, send_index, scaled, pieces_1, 4)
    pieces_2 = gather_whole(after(cut(full_ph, True)[0], pieces_1), outgoing_1)
    came_1 = exchange(outgoing_1)
    phi_2, outgoing_2 = ph_half(True, send_index, scaled, pieces_2, NEAR)
    pp_pieces = gather_rows(*after(pp_halves, pieces_2), between=outgoing_2)
    came_2 = exchange(outgoing_2)
    held = tuple(hold(x, FAR) if k in (1, 2) else x for k, x in enumerate(pp_pieces[2:6]))
    leaving = pp_whole(
        recv_index, came_1, came_2, chi_pp, pp_pieces[:2] + held + pp_pieces[6:]
    )
    base = base_sum(gamma_ph, phi_1, phi_2)
    return last_sum(send_index, base, exchange(leaving))


def solution(mesh):
    placed = (
        P("boson", "block", None),
        P("boson", "block", None),
        P("boson", None),
        P("boson", "block", None),
        P("boson", None),
        P(),
    )
    return jax.shard_map(
        local, mesh=mesh, in_specs=placed, out_specs=P("boson", "block", None), check_vma=False
    )
```

```python
import jax
import jax.numpy as jnp
from jax import lax
from jax.experimental import pallas as pl
from jax.experimental.pallas import tpu as pltpu
from jax.sharding import PartitionSpec as P

CB = 8
RS = 4
CAP = 3
ITEMS = RS * CB
MIB = 1 << 20
NEAR, FAR = 20, 14
BF16 = jnp.bfloat16
F32 = jnp.float32


def low_lanes(rows):
    return lax.broadcasted_iota(jnp.int32, (rows, 128), 1) < 64


def swap_lanes(x):
    return pltpu.roll(x, 64, 1)


def start_all(copies):
    for copy in copies:
        copy.start()
    return copies


def wait_all(copies):
    for copy in copies:
        copy.wait()


def point_loads(sources, targets, sems):
    return [
        start_all(
            [
                pltpu.make_async_copy(x.at[q], y.at[q], sems.at[k, q])
                for k, (x, y) in enumerate(zip(sources, targets))
            ]
        )
        for q in range(4)
    ]


def right_loads(pieces, block_here, right, sems):
    where = [(step, offset) for step in STEPS for offset in (0, 128)]
    where = [(s, o) for k, (s, o) in enumerate(where) if len(pieces) == 8 or o == 0 or k == 7]
    loads = []
    for q in range(4):
        copies = []
        for k, (piece, (step, offset)) in enumerate(zip(pieces, where)):
            start = pl.multiple_of(lax.rem(block_here + step, 4) * 256 + offset, 128)
            to = right.at[q, pl.ds(start, piece.shape[1])]
            copies.append(pltpu.make_async_copy(piece.at[q], to, sems.at[k, q]))
        loads.append(start_all(copies))
    return loads


def cut_kernel(high_lanes, x, *refs):
    n = (len(refs) - 3) // 2
    outs, x_here, outs_here, in_sems, out_sems = refs[:n], refs[n], refs[n + 1 : -2], refs[-2], refs[-1]
    loads = point_loads([x], [x_here], in_sems)
    low = low_lanes(256)
    stores = []
    for q in range(4):
        wait_all(loads[q])
        for m in range(4):
            even = x_here[q, :, m * 256 : m * 256 + 128].astype(F32)
            odd = swap_lanes(x_here[q, :, m * 256 + 128 : m * 256 + 256].astype(F32))
            lanes = jnp.where(low, odd, even) if high_lanes else jnp.where(low, even, odd)
            out = outs_here[m * n // 4]
            to = m * 128 % out.shape[2]
            out[q, :, to : to + 128] = lanes.astype(BF16)
        stores += start_all(
            [
                pltpu.make_async_copy(y.at[q], out.at[q], out_sems.at[k, q])
                for k, (y, out) in enumerate(zip(outs_here, outs))
            ]
        )
    wait_all(stores)


def hold_kernel(x, out):
    pass


def after(value, others):
    return lax.optimization_barrier((value, others))[0]


def gather_rows(low, high, between=None):
    n = lax.axis_size("block")
    up = [(i, (i + 1) % n) for i in range(n)]
    down = [(i, (i - 1) % n) for i in range(n)]
    below_low = lax.ppermute(low, "block", up)
    above_high = lax.ppermute(high, "block", down)
    below_high = lax.ppermute(high, "block", up)
    above_low = lax.ppermute(low, "block", down)
    near = (below_low, above_high)
    if between is not None:
        near = after(near, between)
    far_low = lax.ppermute(near[0], "block", up)
    far_high = lax.ppermute(near[1], "block", down)
    return low, high, below_low, below_high, above_low, above_high, far_low, far_high


def gather_whole(own, between):
    n = lax.axis_size("block")
    up = [(i, (i + 1) % n) for i in range(n)]
    down = [(i, (i - 1) % n) for i in range(n)]
    half = own.shape[1] // 2
    below = lax.ppermute(own, "block", up)
    above = lax.ppermute(own, "block", down)
    near_low, near_high = after((below[:, :half], above[:, half:]), between)
    return (
        own,
        below,
        above,
        lax.ppermute(near_low, "block", up),
        lax.ppermute(near_high, "block", down),
    )


STEPS = (0, 3, 1, 2)


def product(lhs, here, pieces, q, half):
    total = None
    for k, step in enumerate(STEPS):
        start = pl.multiple_of(lax.rem(here + step, 4) * 256, 256)
        block = pieces[2 * k + half][q]
        term = jnp.dot(lhs[:, pl.ds(start, 256)], block, preferred_element_type=F32)
        total = term if total is None else total + term
    return total


def scale_kernel(gamma, chi, out):
    row = chi[pl.ds(pl.program_id(0), 1), :]
    out[0] = (gamma[0].astype(F32) * row).astype(BF16)


def ph_kernel(second, index, scaled, *refs):
    n = 5 if second else 8
    pieces, (phi_out, slots_out, phi, slots, out_sems) = refs[:n], refs[n : n + 5]
    if second:
        left, right, left_sems, in_sems = refs[n + 5 :]
        left_loads = point_loads([scaled], [left], left_sems)
        loads = right_loads(pieces, index[128], right, in_sems)
    low = low_lanes(32)
    stores = []
    for q in range(4):
        if second:
            wait_all(left_loads[q] + loads[q])
        for half in range(2):
            columns = slice(half * 256, half * 256 + 256)
            if second:
                part = jnp.dot(left[q], right[q, :, columns], preferred_element_type=F32)
            else:
                part = product(scaled.at[q], index[128], pieces, q, half)
            phi[q, :, columns] = part
            for r in range(RS):
                for m in range(2):
                    pair = part[r * 64 : r * 64 + 64, m * 128 : m * 128 + 128]
                    top, bottom = pair[:32], swap_lanes(pair[32:])
                    item = q * ITEMS + r * CB + half * 4 + m * 2
                    ahead, behind = (1, 0) if second else (0, 1)
                    slots[index[item + ahead]] = jnp.where(low, top, bottom).astype(BF16)
                    slots[index[item + behind]] = jnp.where(low, bottom, top).astype(BF16)
        stores += start_all([pltpu.make_async_copy(phi.at[q], phi_out.at[q], out_sems.at[q])])
    stores += start_all([pltpu.make_async_copy(slots, slots_out, out_sems.at[4])])
    wait_all(stores)


def unpack_kernel(index, first_in, second, chi, lhs, first, sems):
    wait_all(start_all([pltpu.make_async_copy(first_in, first, sems.at[0])]))
    low = low_lanes(32)
    for p in range(4):
        row = chi[p : p + 1, :]
        for r in range(RS):
            for c in range(CB):
                slot = index[p * ITEMS + r * CB + c]
                a, b = first[slot].astype(F32), second[slot].astype(F32)
                scale = row[:, c * 128 : c * 128 + 128]
                straight = (jnp.where(low, a, b) * scale).astype(BF16)
                crossed = (swap_lanes(jnp.where(low, b, a)) * scale).astype(BF16)
                top = r * 64 + c % 2 * 32
                other = r * 64 + 32 - c % 2 * 32
                lhs[p, top : top + 32, c * 128 : c * 128 + 128] = straight
                lhs[p, other : other + 32, c * 128 : c * 128 + 128] = crossed


def pp_kernel(index, lhs, *refs):
    pieces, slots_out = refs[:8], refs[8]
    right, tiles, in_sems, slot_sems = refs[9:]
    loads = right_loads(pieces, index[128], right, in_sems)
    for p in range(4):
        wait_all(loads[p])
        for half in range(2):
            columns = slice(half * 512, half * 512 + 512)
            phi = jnp.dot(lhs[p], right[p, :, columns], preferred_element_type=F32).astype(BF16)
            for r in range(RS):
                for c in range(4):
                    item = p * ITEMS + r * CB + half * 4 + c
                    tiles[item] = phi[r * 64 : r * 64 + 64, c * 128 : c * 128 + 128]
                    to = slots_out.at[index[item]]
                    pltpu.make_async_copy(tiles.at[item], to, slot_sems.at[0]).start()
    pltpu.make_async_copy(tiles, slots_out.at[: 4 * ITEMS], slot_sems.at[0]).wait()


def base_kernel(gamma, first, second, out):
    low = low_lanes(256)
    for m in range(4):
        a = first[0, :, m * 128 : m * 128 + 128]
        b = second[0, :, m * 128 : m * 128 + 128]
        for c, phi in ((2 * m, jnp.where(low, a, b)), (2 * m + 1, swap_lanes(jnp.where(low, b, a)))):
            columns = slice(c * 128, c * 128 + 128)
            out[0, :, columns] = gamma[0, :, columns].astype(F32) + phi


def sum_kernel(index, base_in, came, out, base, total, in_sems, out_sems):
    loads = point_loads([base_in], [base], in_sems)
    stores = []
    for q in range(4):
        wait_all(loads[q])
        for r in range(RS):
            for c in range(CB):
                rows, columns = slice(r * 64, r * 64 + 64), slice(c * 128, c * 128 + 128)
                back = came[index[q * ITEMS + r * CB + c]].astype(F32)
                total[q, rows, columns] = (base[q, rows, columns] + back).astype(BF16)
        stores += start_all([pltpu.make_async_copy(total.at[q], out.at[q], out_sems.at[q])])
    wait_all(stores)


def point_spec(rows, columns):
    return pl.BlockSpec((1, rows, columns), lambda q, *index: (q, 0, 0))


def whole_spec(shape):
    return pl.BlockSpec(shape, lambda q, *index: (0,) * len(shape))


def call(
    kernel, index, operands, in_specs, out_specs, out_shape, scratch, us, grant, free=(), **other
):
    return pl.pallas_call(
        kernel,
        grid_spec=pltpu.PrefetchScalarGridSpec(
            num_scalar_prefetch=len(index),
            grid=other.get("grid", (4,)),
            in_specs=in_specs,
            out_specs=out_specs,
            scratch_shapes=scratch,
        ),
        out_shape=out_shape,
        compiler_params=pltpu.CompilerParams(vmem_limit_bytes=grant * MIB),
        cost_estimate=pl.CostEstimate(
            flops=int(us * 1e9), bytes_accessed=int(us * 3e6), transcendentals=0
        ),
        input_output_aliases=other.get("aliases", {}),
    )(
        *index,
        *(
            x if k in free else pltpu.with_memory_space_constraint(x, pltpu.HBM)
            for k, x in enumerate(operands)
        ),
    )


def plan(relabel, points, boson_here, block_here):
    nboson = lax.axis_size("boson")
    item_total = points * ITEMS
    own_targets = lax.dynamic_slice(
        relabel, (boson_here * points, block_here * RS, 0), (points, RS, CB)
    ).reshape(item_total)
    shifts = (own_targets // points - boson_here) % nboson
    item_range = jnp.arange(item_total, dtype=jnp.int32)
    target = own_targets % points * ITEMS + item_range % ITEMS
    earlier = (shifts[None, :] == shifts[:, None]) & (item_range[None, :] < item_range[:, None])
    rank = jnp.sum(earlier.astype(jnp.int32), axis=1)
    send = (boson_here + shifts) % nboson * CAP + rank
    recv = (boson_here - shifts) % nboson * CAP + rank
    recv_at = jnp.sum(
        (target[None, :] == item_range[:, None]).astype(jnp.int32) * recv[None, :], axis=1
    )
    return send, recv_at


def exchange(slots):
    nboson = lax.axis_size("boson")
    tile = slots.shape[1:]
    return lax.all_to_all(
        slots.reshape((nboson, CAP) + tile), "boson", split_axis=0, concat_axis=0, tiled=True
    ).reshape(slots.shape)


HALF_TILES = (64 * CAP, 32, 128)
TILES = (64 * CAP, 64, 128)
ROWS = point_spec(256, 1024)
CHI = whole_spec((4, 1024))


def specs(pieces):
    return [point_spec(*x.shape[1:]) for x in pieces]


ANY = pl.BlockSpec(memory_space=pl.ANY)
NEAR_BY = pl.BlockSpec(memory_space=pltpu.VMEM)
DMA = pltpu.SemaphoreType.DMA


def vmem(x):
    return pltpu.VMEM(x.shape, x.dtype)


def cut(full, high_lanes):
    def kernel(*refs):
        cut_kernel(high_lanes, *refs)

    parts = 1 if high_lanes else 2
    shape = (4, 256, 512 // parts)
    scratch = [vmem(full)] + [pltpu.VMEM(shape, BF16)] * parts + [DMA((1, 4)), DMA((parts, 4))]
    outs = [jax.ShapeDtypeStruct(shape, BF16)] * parts
    return call(kernel, (), (full,), [ANY], [ANY] * parts, outs, scratch, 2, 6, grid=())


def scale_rows(gamma, chi):
    out = jax.ShapeDtypeStruct(gamma.shape, BF16)
    return call(scale_kernel, (), (gamma, chi), [ROWS, CHI], ROWS, out, [], 2, 6)


def hold(x, us):
    anywhere = pl.BlockSpec(memory_space=pl.ANY)
    out = pltpu.HBM(x.shape, x.dtype)
    return call(
        hold_kernel, (), (x,), [anywhere], anywhere, out, [], us, 1, grid=(1,), aliases={0: 0}
    )


def ph_half(second, index, scaled, pieces, us):
    def kernel(*refs):
        ph_kernel(second, *refs)

    phi = (4, 256, 512)
    scratch = [pltpu.VMEM(phi, F32), pltpu.VMEM(HALF_TILES, BF16), DMA((5,))]
    if second:
        scratch += [vmem(scaled), pltpu.VMEM((4, 1024, 512), BF16), DMA((1, 4)), DMA((5, 4))]
    return call(
        kernel,
        (index,),
        (scaled,) + pieces,
        [ANY if second else NEAR_BY] * (len(pieces) + 1),
        [ANY] * 2,
        [pltpu.HBM(phi, F32), pltpu.HBM(HALF_TILES, BF16)],
        scratch,
        us,
        14 if second else 8,
        free=() if second else tuple(range(9)),
        grid=(),
    )


def unpack(index, came_1, came_2, chi):
    return call(
        unpack_kernel,
        (index,),
        (came_1, came_2, chi),
        [ANY, NEAR_BY, NEAR_BY],
        NEAR_BY,
        jax.ShapeDtypeStruct((4, 256, 1024), BF16),
        [vmem(came_1), DMA((1,))],
        4,
        8,
        free=(1, 2),
        grid=(),
    )


def pp_whole(index, lhs, pieces):
    scratch = [pltpu.VMEM((4, 1024, 1024), BF16), pltpu.VMEM((4 * ITEMS, 64, 128), BF16)]
    return call(
        pp_kernel,
        (index,),
        (lhs,) + pieces,
        [NEAR_BY] + [ANY] * 8,
        ANY,
        pltpu.HBM(TILES, BF16),
        scratch + [DMA((8, 4)), DMA((1,))],
        5,
        16,
        free=(0, 7, 8),
        grid=(),
    )


def base_sum(gamma, phi_1, phi_2):
    return call(
        base_kernel,
        (),
        (gamma, phi_1, phi_2),
        [ROWS] + [point_spec(256, 512)] * 2,
        ROWS,
        pltpu.HBM(gamma.shape, F32),
        [],
        4,
        10,
    )


def last_sum(index, base, back):
    out = pltpu.HBM(base.shape, BF16)
    scratch = [vmem(base), pltpu.VMEM(base.shape, BF16), DMA((1, 4)), DMA((4,))]
    return call(
        sum_kernel,
        (index,),
        (base, back),
        [ANY, NEAR_BY],
        ANY,
        out,
        scratch,
        3,
        10,
        free=(1,),
        grid=(),
    )


def local(gamma_ph, full_ph, chi_ph, pp_vertex, chi_pp, relabel):
    block_here = lax.axis_index("block")
    send, recv_at = plan(relabel, gamma_ph.shape[0], lax.axis_index("boson"), block_here)
    here = jnp.full((8,), block_here, jnp.int32)
    send_index = jnp.concatenate([send, here])
    recv_index = jnp.concatenate([recv_at, here])

    full_ph, gamma_ph = after((full_ph, gamma_ph), (send_index, recv_index))
    scaled = scale_rows(gamma_ph, chi_ph)
    pp_halves = (pp_vertex[:, :128], pp_vertex[:, 128:])
    pieces_1 = gather_rows(*cut(full_ph, False), between=pp_halves)
    phi_1, outgoing_1 = ph_half(False, send_index, scaled, pieces_1, 4)
    pieces_2 = gather_whole(after(cut(full_ph, True)[0], pieces_1), outgoing_1)
    came_1 = exchange(outgoing_1)
    phi_2, outgoing_2 = ph_half(True, send_index, scaled, pieces_2, NEAR)
    pp_pieces = gather_rows(*after(pp_halves, pieces_2), between=outgoing_2)
    came_2 = exchange(outgoing_2)
    held = tuple(hold(x, FAR) if k in (1, 2) else x for k, x in enumerate(pp_pieces[2:6]))
    lhs = unpack(recv_index, came_1, came_2, chi_pp)
    leaving = pp_whole(recv_index, lhs, pp_pieces[:2] + held + pp_pieces[6:])
    base = base_sum(gamma_ph, phi_1, phi_2)
    return last_sum(send_index, base, exchange(leaving))


def solution(mesh):
    placed = (
        P("boson", "block", None),
        P("boson", "block", None),
        P("boson", None),
        P("boson", "block", None),
        P("boson", None),
        P(),
    )
    return jax.shard_map(
        local, mesh=mesh, in_specs=placed, out_specs=P("boson", "block", None), check_vma=False
    )
```
